128 devices in a mesh: seq: 16 (over x, y), head: 8 (over z, core).
Axes of the slice: x: 4, y: 4, z: 4, core: 2. Of those that a mesh axis runs over, the one named last changes fastest.
Arguments:
- attn_q: bfloat16 [16384, 5120], P('seq', 'head'), may hold values from -6 to 6
- attn_k: bfloat16 [16384, 5120], P('seq', 'head'), may hold values from -6 to 6
- attn_v: bfloat16 [16384, 5120], P('seq', 'head'), may hold values from -6 to 6
- fast_q: bfloat16 [16384, 5120], P('seq', 'head'), may hold values from -6 to 6
- fast_k: bfloat16 [16384, 5120], P('seq', 'head'), may hold values from -6 to 6
- fast_v: bfloat16 [16384, 5120], P('seq', 'head'), may hold values from -6 to 6
- rates: float32 [16384, 8], P('seq', 'head'), may hold values from 0.00015625 to 0.0015625
- fast_gate: float32 [8, 640, 640], P('head'), may hold values from -0.25 to 0.25
- fast_up: float32 [8, 640, 640], P('head'), may hold values from -0.25 to 0.25
- fast_down: float32 [8, 640, 640], P('head'), may hold values from -0.25 to 0.25
Outputs:
- mixed: bfloat16 [16384, 5120], P('seq', 'head')
The draws below stay inside these ranges and needn't reach their ends.
All inputs are finite; a program needn't handle non-finite values.
Results may differ from the reference program's by a relative error of at most 0.012.
Values may be sent and summed in bfloat16 or wider, within the bound.
A program may use at most 128 MiB of HBM per device.

```python
import math
import jax
import jax.numpy as jnp
from jax import lax

HEADS = 40
HD = 128
FW_HEADS = 8
FWD = 640
WINDOW = 1024
TOK_DEV = 1024
TOKENS = 16384
D = 5120


def drawn_pair(key):
    base = jax.random.fold_in(key, 1234)
    key_query, key_keys = jax.random.split(base, 2)
    array_shape = (TOKENS, HEADS * HD)
    queries = jax.random.truncated_normal(key_query, -6.0, 6.0, array_shape, jnp.float32)
    key_rows = jax.random.truncated_normal(key_keys, -6.0, 6.0, array_shape, jnp.float32)
    return (queries, key_rows)


def draw_attn_q(key, part):
    return drawn_pair(key)[0].astype(jnp.bfloat16)


def draw_attn_k(key, part):
    return drawn_pair(key)[1].astype(jnp.bfloat16)


def levels(own_key, extent, cuts, least, high):
    def one(position, shards_of):
        heights = jax.random.uniform(jax.random.fold_in(jax.random.fold_in(own_key, 6), position), (shards_of,), jnp.float32, least / len(cuts), high / len(cuts))
        return jnp.repeat(jnp.exp(heights), extent[position] // shards_of).reshape((-1,) + (1,) * (len(extent) - position - 1))

    factor_of = one(*cuts[0])
    for cut in cuts[1:]:
        factor_of = factor_of * one(*cut)
    return factor_of


def normal_values(key, shape, deviation, limit, pieces=(), kind=jnp.bfloat16):
    values = deviation * jax.random.normal(key, shape, jnp.float32)
    if pieces:
        values = values * levels(key, shape, pieces, -0.22, 0.18)
    return jnp.clip(values, -limit, limit).astype(kind)


def setup_inputs(seed: int = 0) -> dict:
    arg_keys = jax.random.split(jax.random.key(seed), 11)
    attn_q = draw_attn_q(jax.random.fold_in(arg_keys[10], 71), 0)
    attn_k = draw_attn_k(jax.random.fold_in(arg_keys[10], 71), 0)
    attn_v = normal_values(arg_keys[2], (TOKENS, D), 1.0, 6.0, ((0, 16), (1, 8)))
    fast_q = normal_values(arg_keys[3], (TOKENS, D), 1.0, 6.0, ((0, 16), (1, 8)))
    fast_k = normal_values(arg_keys[4], (TOKENS, D), 1.0, 6.0, ((0, 16), (1, 8)))
    fast_v = normal_values(arg_keys[5], (TOKENS, D), 1.0, 6.0, ((0, 16), (1, 8)))
    rates = jnp.clip(jnp.exp(math.log(0.0015625) - 2.3025851 * jax.random.uniform(arg_keys[6], (TOKENS, FW_HEADS), jnp.float32) ** levels(arg_keys[6], (TOKENS, FW_HEADS), ((0, 16), (1, 8)), -0.2, 0.2)), 0.00015625, 0.0015625)
    fast_gate = normal_values(arg_keys[7], (FW_HEADS, FWD, FWD), FWD ** -0.5, 0.25, ((0, 8),), jnp.float32)
    fast_up = normal_values(arg_keys[8], (FW_HEADS, FWD, FWD), FWD ** -0.5, 0.25, ((0, 8),), jnp.float32)
    fast_down = normal_values(arg_keys[9], (FW_HEADS, FWD, FWD), FWD ** -0.5, 0.25, ((0, 8),), jnp.float32)
    return dict(attn_q=attn_q, attn_k=attn_k, attn_v=attn_v, fast_q=fast_q, fast_k=fast_k, fast_v=fast_v, rates=rates, fast_gate=fast_gate, fast_up=fast_up, fast_down=fast_down)


epsilon = 1e-06

def attention(attn_q, attn_k, attn_v):
    block_rows = min(512, TOK_DEV)
    inverse_root = 1.0 / math.sqrt(HD)
    zero_rim = jnp.zeros((WINDOW, HEADS * HD), attn_k.dtype)
    ext_keys = jnp.concatenate([zero_rim, attn_k], axis=0)
    ext_values = jnp.concatenate([zero_rim, attn_v], axis=0)

    def one_block(block_index):
        first_row = (block_index * block_rows).astype(jnp.int32)
        query = lax.dynamic_slice_in_dim(attn_q, first_row, block_rows, 0).astype(jnp.float32).reshape(block_rows, HEADS, HD)
        key_block = lax.dynamic_slice_in_dim(ext_keys, first_row, WINDOW + block_rows, 0).astype(jnp.float32).reshape(WINDOW + block_rows, HEADS, HD)
        value_block = lax.dynamic_slice_in_dim(ext_values, first_row, WINDOW + block_rows, 0).astype(jnp.float32).reshape(WINDOW + block_rows, HEADS, HD)
        scores = jnp.einsum('qhd,khd->hqk', query, key_block, precision=lax.Precision.HIGHEST) * inverse_root
        query_pos = first_row + jnp.arange(block_rows, dtype=jnp.int32)
        key_pos = first_row - WINDOW + jnp.arange(WINDOW + block_rows, dtype=jnp.int32)
        distance = query_pos[:, None] - key_pos[None, :]
        allowed = (distance >= 0) & (distance <= WINDOW) & (key_pos[None, :] >= 0)
        scores = jnp.where(allowed[None], scores, -jnp.inf)
        row_max = lax.optimization_barrier(jnp.max(scores, axis=-1, keepdims=True))
        expo = jnp.exp(scores - row_max)
        weights = (expo / lax.optimization_barrier(jnp.sum(expo, axis=-1, keepdims=True))).astype(jnp.bfloat16)
        result = jnp.einsum('hqk,khd->qhd', weights.astype(jnp.float32), value_block, precision=lax.Precision.HIGHEST)
        return result.reshape(block_rows, HEADS * HD)
    blocks = lax.map(one_block, jnp.arange(TOKENS // block_rows, dtype=jnp.int32))
    return blocks.reshape(TOKENS, HEADS * HD)

def renorm(previous, gradient):
    updated = previous - gradient
    old_norm = jnp.sqrt(lax.optimization_barrier(jnp.sum(previous * previous, axis=-2, keepdims=True)))
    new_norm = jnp.sqrt(lax.optimization_barrier(jnp.sum(updated * updated, axis=-2, keepdims=True)) + epsilon)
    return updated * (old_norm / new_norm)

def reference(attn_q, attn_k, attn_v, fast_q, fast_k, fast_v, rates, fast_gate, fast_up, fast_down):
    attended = attention(attn_q, attn_k, attn_v)
    applied_list = []
    for head_index in range(FW_HEADS):
        cols = slice(head_index * FWD, (head_index + 1) * FWD)
        key_rows = fast_k[:, cols]
        gate_b = fast_gate[head_index].astype(jnp.bfloat16)
        up_b = fast_up[head_index].astype(jnp.bfloat16)
        down_b = fast_down[head_index].astype(jnp.bfloat16)
        pre_gate = jnp.dot(key_rows, gate_b, preferred_element_type=jnp.float32)
        pre_up = jnp.dot(key_rows, up_b, preferred_element_type=jnp.float32)
        activated = jax.nn.silu(pre_gate)
        hidden = (activated * pre_up).astype(jnp.bfloat16)
        out_grad = (-rates[:, head_index:head_index + 1] * fast_v[:, cols].astype(jnp.float32)).astype(jnp.bfloat16)
        hidden_grad = jnp.dot(out_grad, down_b.T, preferred_element_type=jnp.float32)
        sigma = jax.nn.sigmoid(pre_gate)
        gate_grad = (hidden_grad * pre_up * sigma * (1.0 + pre_gate * (1.0 - sigma))).astype(jnp.bfloat16)
        up_grad = (hidden_grad * activated).astype(jnp.bfloat16)
        grad_gate = jnp.dot(key_rows.T, gate_grad, preferred_element_type=jnp.float32)
        grad_up = jnp.dot(key_rows.T, up_grad, preferred_element_type=jnp.float32)
        grad_down = jnp.dot(hidden.T, out_grad, preferred_element_type=jnp.float32)
        new_gate = renorm(fast_gate[head_index], grad_gate).astype(jnp.bfloat16)
        new_up = renorm(fast_up[head_index], grad_up).astype(jnp.bfloat16)
        new_down = renorm(fast_down[head_index], grad_down).astype(jnp.bfloat16)
        query_rows = fast_q[:, cols]
        query_gate = jnp.dot(query_rows, new_gate, preferred_element_type=jnp.float32)
        query_up = jnp.dot(query_rows, new_up, preferred_element_type=jnp.float32)
        query_hidden = (jax.nn.silu(query_gate) * query_up).astype(jnp.bfloat16)
        applied_list.append(jnp.dot(query_hidden, new_down, preferred_element_type=jnp.float32))
    applied = jnp.concatenate(applied_list, axis=1)
    return (attended + applied).astype(jnp.bfloat16)
```

```python
import math

import jax
import jax.numpy as jnp
from jax import lax
from jax.experimental import pallas as pl
from jax.experimental.pallas import tpu as pltpu
from jax.sharding import PartitionSpec as P

HD = 128
FWD = 640
TOK = 1024
HEADS = 5
QB = 256
TB = 512
EPS = 1e-06
MESH = pl.DeviceIdType.MESH
SCALE = math.log2(math.e) / math.sqrt(HD)
NEG = -1e30
BF = jnp.bfloat16
F32 = jnp.float32

CHUNKS = ((0, 256, "x"), (256, 256, "y"), (512, 128, "x"))


class Remote:
    def __init__(self, src, dst, send_sem, recv_sem, device):
        self.parts = src, dst, send_sem, recv_sem
        self.device = device

    def copy(self):
        return pltpu.make_async_remote_copy(
            *self.parts, device_id=self.device, device_id_type=MESH
        )

    def start(self):
        self.copy().start()

    def wait_recv(self):
        self.copy().wait_recv()

    def wait_send(self):
        self.copy().wait_send()


def up16(n):
    return (n + 15) // 16 * 16


def nt(a, b):
    return lax.dot_general(a, b, (((1,), (1,)), ((), ())), preferred_element_type=F32)


def nn(a, b):
    return lax.dot_general(a, b, (((1,), (0,)), ((), ())), preferred_element_type=F32)


def kernel(
    aq, ak, av, fq, fk, fv, rt, w1, w3, w2, out,
    aq_v, ak_v, av_v, fq_v, fk_v, fv_v, rt_v, w1_v, w3_v, w2_v,
    mstack, mbf, gsum, gbf, rx0, rx1, rx2, fb0, fb1, fb2, part, share_out, share_in,
    new_out, new_in, nstack, qn, o_send, o_recv, o_own, lse_own, lse_nb, lse_send, lse_recv,
    acc, ld_sem, q_ss, q_rs, o_ss, o_rs, l_ss, l_rs, c_ss, c_rs,
):
    seq = lax.axis_index("seq")
    head = lax.axis_index("head")
    cx = seq // 4
    cy = lax.rem(seq, 4)
    rx = (rx0, rx1, rx2)
    fb = (fb0, fb1, fb2)

    def at(axis, d):
        if axis == "x":
            return (lax.rem(cx + d + 4, 4) * 4 + cy, head)
        return (cx * 4 + lax.rem(cy + d + 4, 4), head)

    def coord(axis, d=0):
        return lax.rem((cx if axis == "x" else cy) + d + 4, 4)

    before = (lax.rem(seq + 15, 16), head)
    after = (lax.rem(seq + 1, 16), head)

    loads = []
    for i, (src, dst) in enumerate(
        (
            (w1, w1_v), (w3, w3_v), (w2, w2_v), (fk, fk_v), (fv, fv_v), (rt, rt_v),
            (ak, ak_v), (av, av_v), (aq, aq_v), (fq, fq_v),
        )
    ):
        c = pltpu.make_async_copy(src, dst, ld_sem.at[i])
        c.start()
        loads.append(c)

    barrier = pltpu.get_barrier_semaphore()
    peers = [at(a, d) for a in ("x", "y") for d in (1, -1, 2)] + [before, after]
    for p in peers:
        pl.semaphore_signal(barrier, inc=1, device_id=p, device_id_type=MESH)
    pl.semaphore_wait(barrier, len(peers))

    def lanes(h):
        if isinstance(h, int):
            return pl.ds(h * HD, HD)
        return pl.ds(pl.multiple_of(h * HD, HD), HD)

    def q_copy(h):
        return Remote(aq.at[:, lanes(h)], qn.at[h], q_ss.at[h], q_rs.at[h], before)

    def o_copy(h):
        return Remote(o_send.at[h], o_recv.at[h], o_ss.at[h], o_rs.at[h], after)

    def lse_copy():
        return Remote(lse_send, lse_recv, l_ss.at[0], l_rs.at[0], after)

    for h in range(HEADS):
        q_copy(h).start()

    def sizes(c):
        first, width, axis = CHUNKS[c]
        rows = 3 * width
        return 3 * first, width, rows, rows // 4, rows // 8, rows // 16, axis, "y" if axis == "x" else "x"

    def rows_of(base, index, n):
        return pl.ds(pl.multiple_of(base + index * n, 8 if n % 16 else 16), n)

    def rs1_copies(c):
        base, _, _, p, hf, _, a, _ = sizes(c)
        up, dn, op = coord(a, 1), coord(a, -1), coord(a, 2)
        ss, rs, r = c_ss.at[c], c_rs.at[c], rx[c]
        return (
            Remote(gbf.at[rows_of(base, op * 2, hf)], r.at[0], ss.at[0], rs.at[0], at(a, 1)),
            Remote(gbf.at[rows_of(base, op * 2 + 1, hf)], r.at[1], ss.at[1], rs.at[1], at(a, -1)),
            Remote(gbf.at[rows_of(base, up * 2 + 1, hf)], r.at[2], ss.at[2], rs.at[2], at(a, 1)),
            Remote(gbf.at[rows_of(base, dn * 2, hf)], r.at[3], ss.at[3], rs.at[3], at(a, -1)),
            Remote(fb[c].at[0], r.at[4], ss.at[4], rs.at[4], at(a, 1)),
            Remote(fb[c].at[1], r.at[5], ss.at[5], rs.at[5], at(a, -1)),
        )

    def rs1_start(c):
        for cp in rs1_copies(c)[:4]:
            cp.start()

    def rs1_mid(c):
        base, _, _, _, hf, _, a, _ = sizes(c)
        cps = rs1_copies(c)
        cps[0].wait_recv()
        fb[c][0] = (gsum[rows_of(base, coord(a, 1) * 2, hf), :] + rx[c][0].astype(F32)).astype(BF)
        cps[4].start()
        cps[1].wait_recv()
        fb[c][1] = (gsum[rows_of(base, coord(a, -1) * 2 + 1, hf), :] + rx[c][1].astype(F32)).astype(BF)
        cps[5].start()

    def rs2_copies(c):
        _, _, _, _, _, s, _, b = sizes(c)
        s = up16(s)
        ss, rs = c_ss.at[c], c_rs.at[c]
        return [
            Remote(
                share_out.at[c, d - 1, pl.ds(0, s)], share_in.at[c, d - 1, pl.ds(0, s)],
                ss.at[5 + d], rs.at[5 + d], at(b, d),
            )
            for d in (1, 2, 3)
        ]

    def rs1_end(c):
        base, _, _, p, hf, s, a, b = sizes(c)
        cps = rs1_copies(c)
        for i in (2, 3, 4, 5):
            cps[i].wait_recv()
        r = rx[c]
        mine = coord(a)
        part[pl.ds(0, hf), :] = (
            gsum[rows_of(base, mine * 2, hf), :] + r[3].astype(F32) + r[4].astype(F32)
        )
        part[pl.ds(hf, hf), :] = (
            gsum[rows_of(base, mine * 2 + 1, hf), :] + r[2].astype(F32) + r[5].astype(F32)
        )
        for d, cp in zip((1, 2, 3), rs2_copies(c)):
            share_out[c, d - 1, pl.ds(0, s), :] = part[rows_of(0, coord(b, d), s), :].astype(BF)
            cp.start()
        gsum[pl.ds(base, s), :] = part[rows_of(0, coord(b), s), :]

    def ag2_copies(c):
        _, _, _, _, _, s, _, b = sizes(c)
        s = up16(s)
        ss, rs = c_ss.at[c], c_rs.at[c]
        return [
            Remote(
                new_out.at[c, pl.ds(0, s)], new_in.at[c, d - 1, pl.ds(0, s)],
                ss.at[8 + d], rs.at[8 + d], at(b, d),
            )
            for d in (1, 2, 3)
        ]

    def rs2_end(c):
        base, width, _, p, _, s, a, b = sizes(c)
        for cp in rs2_copies(c):
            cp.wait_recv()
        total = gsum[pl.ds(base, s), :]
        for d in range(3):
            total = total + share_in[c, d, pl.ds(0, s), :].astype(F32)
        start = coord(a) * p + coord(b) * s
        old = mstack[pl.ds(pl.multiple_of(base + start, 8), s), :]
        new = old - total
        old_norm = jnp.sqrt(jnp.sum(old * old, axis=1, keepdims=True))
        new_norm = jnp.sqrt(jnp.sum(new * new, axis=1, keepdims=True) + EPS)
        row = start + lax.broadcasted_iota(jnp.int32, (s, 1), 0)
        factor = jnp.where(row < 2 * width, old_norm / new_norm, 1.0)
        new_out[c, pl.ds(0, s), :] = (new * factor).astype(BF)
        for cp in ag2_copies(c):
            cp.start()

    def ag1_copies(c):
        base, _, _, p, hf, _, a, _ = sizes(c)
        ss, rs = c_ss.at[c], c_rs.at[c]
        me, dn, up = coord(a), coord(a, -1), coord(a, 1)

        def same(rows, i, d):
            return Remote(nstack.at[rows], nstack.at[rows], ss.at[i], rs.at[i], at(a, d))

        return (
            same(rows_of(base, me, p), 12, 1),
            same(rows_of(base, me, p), 13, -1),
            same(rows_of(base, dn * 2, hf), 14, 1),
            same(rows_of(base, up * 2 + 1, hf), 15, -1),
        )

    def ag2_end(c):
        base, _, _, p, _, s, a, b = sizes(c)
        for cp in ag2_copies(c):
            cp.wait_recv()
        part[rows_of(0, coord(b), s), :] = new_out[c, pl.ds(0, s), :].astype(F32)
        for d in (1, 2, 3):
            part[rows_of(0, coord(b, -d), s), :] = new_in[c, d - 1, pl.ds(0, s), :].astype(F32)
        nstack[rows_of(base, coord(a), p), :] = part[pl.ds(0, p), :].astype(BF)
        cps = ag1_copies(c)
        cps[0].start()
        cps[1].start()

    def ag1_fwd(c):
        cps = ag1_copies(c)
        cps[0].wait_recv()
        cps[2].start()
        cps[1].wait_recv()
        cps[3].start()

    def ag1_end(c):
        cps = ag1_copies(c)
        cps[2].wait_recv()
        cps[3].wait_recv()

    def prepare(c):
        first, width, _ = CHUNKS[c]
        base = 3 * first
        for k in range(width // 128):
            cols = pl.ds(first + k * 128, 128)
            for n, ref in ((0, w1_v), (1, w3_v)):
                t = ref[:, cols].T
                mstack[pl.ds(base + n * width + k * 128, 128), :] = t
                mbf[pl.ds(base + n * width + k * 128, 128), :] = t.astype(BF)
        t = w2_v[pl.ds(first, width), :]
        mstack[pl.ds(base + 2 * width, width), :] = t
        mbf[pl.ds(base + 2 * width, width), :] = t.astype(BF)

    def grads(c):
        first, width, _ = CHUNKS[c]
        base = 3 * first
        rows = [pl.ds(base + n * width, width) for n in range(3)]

        def tokens(i, _):
            tok = pl.ds(pl.multiple_of(i * TB, TB), TB)
            key = fk_v[tok, :]
            og = fv_v[tok, :]
            pg = nt(mbf[rows[0], :], key)
            pu = nt(mbf[rows[1], :], key)
            hg = nt(mbf[rows[2], :], og)
            sg = jax.nn.sigmoid(pg)
            act = pg * sg
            hidden = (act * pu).astype(BF)
            gg = (hg * pu * sg * (1.0 + pg * (1.0 - sg))).astype(BF)
            ug = (hg * act).astype(BF)
            for r, lhs, rhs in ((rows[0], gg, key), (rows[1], ug, key), (rows[2], hidden, og)):
                gsum[r, :] += nn(lhs, rhs)
            return 0

        for r in rows:
            gsum[r, :] = jnp.zeros((width, FWD), F32)
        lax.fori_loop(0, TOK // TB, tokens, 0)
        whole = pl.ds(base, 3 * width)
        gbf[whole, :] = gsum[whole, :].astype(BF)

    for c in loads[:6]:
        c.wait()
    for i in range(TOK // QB):
        tok = pl.ds(i * QB, QB)
        fv_v[tok, :] = (-rt_v[tok, :] * fv_v[tok, :].astype(F32)).astype(BF)
    for c in range(len(CHUNKS)):
        prepare(c)
        grads(c)
        rs1_start(c)
        if c:
            rs1_mid(c - 1)

    for c in loads[6:]:
        c.wait()
    row_i = lax.broadcasted_iota(jnp.int32, (QB, QB), 0)
    col_i = lax.broadcasted_iota(jnp.int32, (QB, QB), 1)
    lane_i = lax.broadcasted_iota(jnp.int32, (QB, HD), 1)

    def attend(q, h, i, own, lse_ref):
        diag = pl.ds(i * QB, QB)
        if own:
            lo, n = 0, i * QB
        else:
            lo, n = (i + 1) * QB, TOK - (i + 1) * QB
        sd = nt(q, ak_v[diag, lanes(h)])
        sd = jnp.where((col_i <= row_i) if own else (col_i >= row_i), sd, NEG)
        m = jnp.max(sd, axis=1, keepdims=True)
        if n:
            so = nt(q, ak_v[pl.ds(lo, n), lanes(h)])
            m = jnp.maximum(m, jnp.max(so, axis=1, keepdims=True))
        pd = jnp.exp2((sd - m) * SCALE)
        l = jnp.sum(pd, axis=1, keepdims=True)
        o = nn(pd.astype(BF), av_v[diag, lanes(h)])
        if n:
            po = jnp.exp2((so - m) * SCALE)
            l = l + jnp.sum(po, axis=1, keepdims=True)
            o = o + nn(po.astype(BF), av_v[pl.ds(lo, n), lanes(h)])
        lse = m * SCALE + jnp.log2(l)
        lse_ref[diag, :] = jnp.where(lane_i == h, lse, lse_ref[diag, :])
        return o / l

    def own(h):
        for i in range(TOK // QB):
            tok = pl.ds(i * QB, QB)
            o_own[tok, lanes(h)] = attend(aq_v[tok, lanes(h)], h, i, True, lse_own).astype(BF)

    def serve(h):
        q_copy(h).wait_recv()
        for i in range(TOK // QB):
            tok = pl.ds(i * QB, QB)
            o_send[h, tok, :] = attend(qn[h, tok, :], h, i, False, lse_nb).astype(BF)
        o_copy(h).start()

    lse_own[...] = jnp.zeros_like(lse_own)
    lse_nb[...] = jnp.zeros_like(lse_nb)

    def when(h, k, *stages):
        @pl.when(h == k)
        def _():
            for f, c in stages:
                f(c)

    def one_head(h, _):
        own(h)
        when(h, 0, (rs1_mid, 2))
        when(h, 1, (rs1_end, 1))
        when(h, 2, (rs2_end, 1))
        when(h, 3, (ag2_end, 1))
        when(h, 4, (ag2_end, 2), (ag1_fwd, 0))
        serve(h)
        when(h, 0, (rs1_end, 0))
        when(h, 1, (rs2_end, 0), (rs1_end, 2))
        when(h, 2, (ag2_end, 0), (rs2_end, 2))
        return 0

    lax.fori_loop(0, HEADS, one_head, 0)
    ag1_fwd(1)
    for i in range(TOK // HD):
        lse_send[:, pl.ds(i * HD, HD)] = lse_nb[pl.ds(i * HD, HD), :].T[0:8, :]
    lse_copy().start()
    ag1_fwd(2)

    def apply(c, first):
        base, width, *_ = sizes(c)

        def tokens(i, _):
            tok = pl.ds(pl.multiple_of(i * QB, QB), QB)
            q = fq_v[tok, :]
            pg = nt(q, nstack[pl.ds(base, width), :])
            pu = nt(q, nstack[pl.ds(base + width, width), :])
            hid = (pg * jax.nn.sigmoid(pg) * pu).astype(BF)
            o = nn(hid, nstack[pl.ds(base + 2 * width, width), :])
            if first:
                acc[tok, :] = o
            else:
                acc[tok, :] += o
            return 0

        lax.fori_loop(0, TOK // QB, tokens, 0)

    new_sq = jnp.zeros((1, FWD), F32)
    for c in range(len(CHUNKS)):
        ag1_end(c)
        apply(c, c == 0)
        base, width, *_ = sizes(c)
        u = nstack[pl.ds(base + 2 * width, width), :].astype(F32)
        new_sq = new_sq + jnp.sum(u * u, axis=0, keepdims=True)
    old = w2_v[...]
    factor = jnp.sqrt(jnp.sum(old * old, axis=0, keepdims=True)) / jnp.sqrt(new_sq + EPS)

    for h in range(HEADS):
        o_copy(h).wait_recv()
    lse_copy().wait_recv()
    for i in range(TOK // HD):
        tok = pl.ds(i * HD, HD)
        theirs = jnp.concatenate([lse_recv[:, tok], jnp.zeros((HD - 8, HD), F32)], axis=0).T
        theirs = jnp.where(seq == 0, NEG, theirs)
        keep = 1.0 / (1.0 + jnp.exp2(theirs - lse_own[tok, :]))
        for h in range(HEADS):
            k = keep[:, h : h + 1]
            o = o_own[tok, lanes(h)].astype(F32) * k + o_recv[h, tok, :].astype(F32) * (1.0 - k)
            out[tok, lanes(h)] = (o + acc[tok, lanes(h)] * factor[:, h * HD : (h + 1) * HD]).astype(BF)

    for h in range(HEADS):
        q_copy(h).wait_send()
        o_copy(h).wait_send()
    lse_copy().wait_send()
    for c in range(len(CHUNKS)):
        for cp in (*rs1_copies(c), *rs2_copies(c), *ag2_copies(c), *ag1_copies(c)):
            cp.wait_send()


def shards(attn_q, attn_k, attn_v, fast_q, fast_k, fast_v, rates, fast_gate, fast_up, fast_down):
    rows = TOK
    act = pltpu.VMEM((rows, FWD), BF)
    weight = pltpu.VMEM((FWD, FWD), F32)
    n = len(CHUNKS)
    half = [3 * w // 8 for _, w, _ in CHUNKS]
    share = max(up16(3 * w // 16) for _, w, _ in CHUNKS)
    scratch = [
        act, act, act, act, act, act, pltpu.VMEM((rows, 1), F32), weight, weight, weight,
        pltpu.VMEM((3 * FWD, FWD), F32),
        pltpu.VMEM((3 * FWD, FWD), BF),
        pltpu.VMEM((3 * FWD, FWD), F32),
        pltpu.VMEM((3 * FWD, FWD), BF),
        *[pltpu.VMEM((6, h, FWD), BF) for h in half],
        *[pltpu.VMEM((2, h, FWD), BF) for h in half],
        pltpu.VMEM((2 * max(half), FWD), F32),
        pltpu.VMEM((n, 3, share, FWD), BF),
        pltpu.VMEM((n, 3, share, FWD), BF),
        pltpu.VMEM((n, share, FWD), BF),
        pltpu.VMEM((n, 3, share, FWD), BF),
        pltpu.VMEM((3 * FWD, FWD), BF),
        pltpu.VMEM((HEADS, rows, HD), BF),
        pltpu.VMEM((HEADS, rows, HD), BF),
        pltpu.VMEM((HEADS, rows, HD), BF),
        act,
        pltpu.VMEM((rows, HD), F32),
        pltpu.VMEM((rows, HD), F32),
        pltpu.VMEM((8, rows), F32),
        pltpu.VMEM((8, rows), F32),
        pltpu.VMEM((rows, FWD), F32),
        pltpu.SemaphoreType.DMA((10,)),
        pltpu.SemaphoreType.DMA((HEADS,)),
        pltpu.SemaphoreType.DMA((HEADS,)),
        pltpu.SemaphoreType.DMA((HEADS,)),
        pltpu.SemaphoreType.DMA((HEADS,)),
        pltpu.SemaphoreType.DMA((1,)),
        pltpu.SemaphoreType.DMA((1,)),
        pltpu.SemaphoreType.DMA((n, 16)),
        pltpu.SemaphoreType.DMA((n, 16)),
    ]
    square = fast_gate.reshape(FWD, FWD), fast_up.reshape(FWD, FWD), fast_down.reshape(FWD, FWD)
    return pl.pallas_call(
        kernel,
        out_shape=jax.ShapeDtypeStruct((rows, FWD), BF),
        in_specs=[pl.BlockSpec(memory_space=pl.ANY)] * 10,
        out_specs=pl.BlockSpec(memory_space=pltpu.VMEM),
        scratch_shapes=scratch,
        compiler_params=pltpu.CompilerParams(
            collective_id=0, has_side_effects=True, vmem_limit_bytes=60 << 20
        ),
    )(attn_q, attn_k, attn_v, fast_q, fast_k, fast_v, rates, *square)


def solution(mesh):
    placed = (P("seq", "head"),) * 7 + (P("head", None, None),) * 3
    return jax.shard_map(
        shards, mesh=mesh, in_specs=placed, out_specs=P("seq", "head"), check_vma=False
    )
```

```python
import math

import jax
import jax.numpy as jnp
from jax import lax
from jax.experimental import pallas as pl
from jax.experimental.pallas import tpu as pltpu
from jax.sharding import PartitionSpec as P

HD = 128
FWD = 640
TOK = 1024
HEADS = 5
QB = 256
TB = 512
EPS = 1e-06
MESH = pl.DeviceIdType.MESH
SCALE = math.log2(math.e) / math.sqrt(HD)
NEG = -1e30
BF = jnp.bfloat16
F32 = jnp.float32

CHUNKS = ((0, 256, "x"), (256, 256, "y"), (512, 128, "x"))


class Remote:
    def __init__(self, src, dst, send_sem, recv_sem, device):
        self.parts = src, dst, send_sem, recv_sem
        self.device = device

    def copy(self):
        return pltpu.make_async_remote_copy(
            *self.parts, device_id=self.device, device_id_type=MESH
        )

    def start(self):
        self.copy().start()

    def wait_recv(self):
        self.copy().wait_recv()

    def wait_send(self):
        self.copy().wait_send()


ORDER = (
    "q31", "v40", "q30", "G2", "q11", "v41", "o40", "q21", "G1", "G0", "s11", "o00",
    "m2", "o20", "q20", "q01", "s40", "o30", "o01", "s31", "m0", "m1", "o21", "s30",
    "e2", "o11", "s41", "e1", "e0", "s01", "q00", "r2", "r1", "r0", "s20", "q10",
    "a2", "a1", "o10", "o31", "a0", "f2", "f1", "f0", "s21", "o41", "s10", "s00",
    "P1", "P0", "M", "P2",
)
KV_HEADS = 1
SERVED = HEADS - KV_HEADS


def up16(n):
    return (n + 15) // 16 * 16


def nt(a, b):
    return lax.dot_general(a, b, (((1,), (1,)), ((), ())), preferred_element_type=F32)


def nn(a, b):
    return lax.dot_general(a, b, (((1,), (0,)), ((), ())), preferred_element_type=F32)


def kernel(
    aq, ak, av, fq, fk, fv, rt, w1, w3, w2, out,
    aq_v, ak_v, av_v, fq_v, fk_v, fv_v, rt_v, w1_v, w3_v, w2_v,
    mstack, mbf, gsum, gbf, rx0, rx1, rx2, fb0, fb1, fb2, part, share_out, share_in,
    new_out, new_in, nstack, qn, kn, vn, o_send, o_recv, o_own, lse_own, lse_nb, lse_kv, lse_send, lse_recv,
    acc, ld_sem, q_ss, q_rs, o_ss, o_rs, k_ss, k_rs, l_ss, l_rs, c_ss, c_rs,
):
    seq = lax.axis_index("seq")
    head = lax.axis_index("head")
    cx = seq // 4
    cy = lax.rem(seq, 4)
    rx = (rx0, rx1, rx2)
    fb = (fb0, fb1, fb2)

    def at(axis, d):
        if axis == "x":
            return (lax.rem(cx + d + 4, 4) * 4 + cy, head)
        return (cx * 4 + lax.rem(cy + d + 4, 4), head)

    def coord(axis, d=0):
        return lax.rem((cx if axis == "x" else cy) + d + 4, 4)

    before = (lax.rem(seq + 15, 16), head)
    after = (lax.rem(seq + 1, 16), head)

    loads = []
    for i, (src, dst) in enumerate(
        (
            (w1, w1_v), (w3, w3_v), (w2, w2_v), (fk, fk_v), (fv, fv_v), (rt, rt_v),
            (ak, ak_v), (av, av_v), (aq, aq_v), (fq, fq_v),
        )
    ):
        c = pltpu.make_async_copy(src, dst, ld_sem.at[i])
        c.start()
        loads.append(c)

    barrier = pltpu.get_barrier_semaphore()
    peers = [at(a, d) for a in ("x", "y") for d in (1, -1, 2)] + [before, after]
    for p in peers:
        pl.semaphore_signal(barrier, inc=1, device_id=p, device_id_type=MESH)
    pl.semaphore_wait(barrier, len(peers))

    def lanes(h):
        if isinstance(h, int):
            return pl.ds(h * HD, HD)
        return pl.ds(pl.multiple_of(h * HD, HD), HD)

    def half(b):
        return pl.ds(b * TOK // 2, TOK // 2)

    def q_copy(h, b):
        return Remote(
            aq.at[half(b), lanes(h)], qn.at[h, half(b)], q_ss.at[h, b], q_rs.at[h, b], before
        )

    def o_copy(h, b):
        return Remote(
            o_send.at[h, half(b)], o_recv.at[h, half(b)], o_ss.at[h, b], o_rs.at[h, b], after
        )

    def kv_copies(h, b):
        n = h - SERVED
        return [
            Remote(
                src.at[half(b), lanes(h)], dst.at[n, half(b)],
                k_ss.at[n, b, i], k_rs.at[n, b, i], after,
            )
            for i, (src, dst) in enumerate(((ak, kn), (av, vn)))
        ]

    def lse_copy():
        return Remote(lse_send, lse_recv, l_ss.at[0], l_rs.at[0], after)

    def sizes(c):
        first, width, axis = CHUNKS[c]
        rows = 3 * width
        return 3 * first, width, rows, rows // 4, rows // 8, rows // 16, axis, "y" if axis == "x" else "x"

    def rows_of(base, index, n):
        return pl.ds(pl.multiple_of(base + index * n, 8 if n % 16 else 16), n)

    def rs1_copies(c):
        base, _, _, p, hf, _, a, _ = sizes(c)
        up, dn, op = coord(a, 1), coord(a, -1), coord(a, 2)
        ss, rs, r = c_ss.at[c], c_rs.at[c], rx[c]
        return (
            Remote(gbf.at[rows_of(base, op * 2, hf)], r.at[0], ss.at[0], rs.at[0], at(a, 1)),
            Remote(gbf.at[rows_of(base, op * 2 + 1, hf)], r.at[1], ss.at[1], rs.at[1], at(a, -1)),
            Remote(gbf.at[rows_of(base, up * 2 + 1, hf)], r.at[2], ss.at[2], rs.at[2], at(a, 1)),
            Remote(gbf.at[rows_of(base, dn * 2, hf)], r.at[3], ss.at[3], rs.at[3], at(a, -1)),
            Remote(fb[c].at[0], r.at[4], ss.at[4], rs.at[4], at(a, 1)),
            Remote(fb[c].at[1], r.at[5], ss.at[5], rs.at[5], at(a, -1)),
        )

    def rs1_start(c):
        for cp in rs1_copies(c)[:4]:
            cp.start()

    def rs1_mid(c):
        base, _, _, _, hf, _, a, _ = sizes(c)
        cps = rs1_copies(c)
        cps[0].wait_recv()
        fb[c][0] = (gsum[rows_of(base, coord(a, 1) * 2, hf), :] + rx[c][0].astype(F32)).astype(BF)
        cps[4].start()
        cps[1].wait_recv()
        fb[c][1] = (gsum[rows_of(base, coord(a, -1) * 2 + 1, hf), :] + rx[c][1].astype(F32)).astype(BF)
        cps[5].start()

    def rs2_copies(c):
        _, _, _, _, _, s, _, b = sizes(c)
        s = up16(s)
        ss, rs = c_ss.at[c], c_rs.at[c]
        return [
            Remote(
                share_out.at[c, d - 1, pl.ds(0, s)], share_in.at[c, d - 1, pl.ds(0, s)],
                ss.at[5 + d], rs.at[5 + d], at(b, d),
            )
            for d in (1, 2, 3)
        ]

    def rs1_end(c):
        base, _, _, p, hf, s, a, b = sizes(c)
        cps = rs1_copies(c)
        for i in (2, 3, 4, 5):
            cps[i].wait_recv()
        r = rx[c]
        mine = coord(a)
        part[pl.ds(0, hf), :] = (
            gsum[rows_of(base, mine * 2, hf), :] + r[3].astype(F32) + r[4].astype(F32)
        )
        part[pl.ds(hf, hf), :] = (
            gsum[rows_of(base, mine * 2 + 1, hf), :] + r[2].astype(F32) + r[5].astype(F32)
        )
        for d, cp in zip((1, 2, 3), rs2_copies(c)):
            share_out[c, d - 1, pl.ds(0, s), :] = part[rows_of(0, coord(b, d), s), :].astype(BF)
            cp.start()
        gsum[pl.ds(base, s), :] = part[rows_of(0, coord(b), s), :]

    def ag2_copies(c):
        _, _, _, _, _, s, _, b = sizes(c)
        s = up16(s)
        ss, rs = c_ss.at[c], c_rs.at[c]
        return [
            Remote(
                new_out.at[c, pl.ds(0, s)], new_in.at[c, d - 1, pl.ds(0, s)],
                ss.at[8 + d], rs.at[8 + d], at(b, d),
            )
            for d in (1, 2, 3)
        ]

    def rs2_end(c):
        base, width, _, p, _, s, a, b = sizes(c)
        for cp in rs2_copies(c):
            cp.wait_recv()
        total = gsum[pl.ds(base, s), :]
        for d in range(3):
            total = total + share_in[c, d, pl.ds(0, s), :].astype(F32)
        start = coord(a) * p + coord(b) * s
        old = mstack[pl.ds(pl.multiple_of(base + start, 8), s), :]
        new = old - total
        old_norm = jnp.sqrt(jnp.sum(old * old, axis=1, keepdims=True))
        new_norm = jnp.sqrt(jnp.sum(new * new, axis=1, keepdims=True) + EPS)
        row = start + lax.broadcasted_iota(jnp.int32, (s, 1), 0)
        factor = jnp.where(row < 2 * width, old_norm / new_norm, 1.0)
        new_out[c, pl.ds(0, s), :] = (new * factor).astype(BF)
        for cp in ag2_copies(c):
            cp.start()

    def ag1_copies(c):
        base, _, _, p, hf, _, a, _ = sizes(c)
        ss, rs = c_ss.at[c], c_rs.at[c]
        me, dn, up = coord(a), coord(a, -1), coord(a, 1)

        def same(rows, i, d):
            return Remote(nstack.at[rows], nstack.at[rows], ss.at[i], rs.at[i], at(a, d))

        return (
            same(rows_of(base, me * 2, hf), 12, 1),
            same(rows_of(base, me * 2 + 1, hf), 13, -1),
            same(rows_of(base, me * 2 + 1, hf), 16, 1),
            same(rows_of(base, me * 2, hf), 17, -1),
            same(rows_of(base, dn * 2, hf), 14, 1),
            same(rows_of(base, up * 2 + 1, hf), 15, -1),
        )

    def ag2_end(c):
        base, _, _, p, _, s, a, b = sizes(c)
        for cp in ag2_copies(c):
            cp.wait_recv()
        part[rows_of(0, coord(b), s), :] = new_out[c, pl.ds(0, s), :].astype(F32)
        for d in (1, 2, 3):
            part[rows_of(0, coord(b, -d), s), :] = new_in[c, d - 1, pl.ds(0, s), :].astype(F32)
        nstack[rows_of(base, coord(a), p), :] = part[pl.ds(0, p), :].astype(BF)
        for cp in ag1_copies(c)[:4]:
            cp.start()

    def ag1_fwd(c):
        cps = ag1_copies(c)
        cps[0].wait_recv()
        cps[4].start()
        cps[1].wait_recv()
        cps[5].start()

    def ag1_end(c):
        cps = ag1_copies(c)
        for cp in cps[2:]:
            cp.wait_recv()

    def prepare(c):
        first, width, _ = CHUNKS[c]
        base = 3 * first
        for k in range(width // 128):
            cols = pl.ds(first + k * 128, 128)
            for n, ref in ((0, w1_v), (1, w3_v)):
                t = ref[:, cols].T
                mstack[pl.ds(base + n * width + k * 128, 128), :] = t
                mbf[pl.ds(base + n * width + k * 128, 128), :] = t.astype(BF)
        t = w2_v[pl.ds(first, width), :]
        mstack[pl.ds(base + 2 * width, width), :] = t
        mbf[pl.ds(base + 2 * width, width), :] = t.astype(BF)

    def grads(c):
        first, width, _ = CHUNKS[c]
        base = 3 * first
        rows = [pl.ds(base + n * width, width) for n in range(3)]

        def tokens(i, _):
            tok = pl.ds(pl.multiple_of(i * TB, TB), TB)
            key = fk_v[tok, :]
            val = fv_v[tok, :]
            rate = -rt_v[:, tok]
            pg = nt(mbf[rows[0], :], key)
            pu = nt(mbf[rows[1], :], key)
            hg = nt(mbf[rows[2], :], val) * rate
            sg = jax.nn.sigmoid(pg)
            act = pg * sg
            hidden = (act * pu * rate).astype(BF)
            gg = (hg * pu * sg * (1.0 + pg * (1.0 - sg))).astype(BF)
            ug = (hg * act).astype(BF)
            for r, lhs, rhs in ((rows[0], gg, key), (rows[1], ug, key), (rows[2], hidden, val)):
                gsum[r, :] += nn(lhs, rhs)
            return 0

        for r in rows:
            gsum[r, :] = jnp.zeros((width, FWD), F32)
        lax.fori_loop(0, TOK // TB, tokens, 0)
        whole = pl.ds(base, 3 * width)
        gbf[whole, :] = gsum[whole, :].astype(BF)

    row_i = lax.broadcasted_iota(jnp.int32, (QB, QB), 0)
    col_i = lax.broadcasted_iota(jnp.int32, (QB, QB), 1)

    def attend(q, keys, vals, i, own, lse_ref, h):
        diag = pl.ds(i * QB, QB)
        if own:
            lo, n = 0, i * QB
        else:
            lo, n = (i + 1) * QB, TOK - (i + 1) * QB
        sd = nt(q, keys(diag))
        sd = jnp.where((col_i <= row_i) if own else (col_i >= row_i), sd, NEG)
        m = jnp.max(sd, axis=1, keepdims=True)
        if n:
            so = nt(q, keys(pl.ds(lo, n)))
            m = jnp.maximum(m, jnp.max(so, axis=1, keepdims=True))
        pd = jnp.exp2((sd - m) * SCALE)
        l = jnp.sum(pd, axis=1, keepdims=True)
        o = nn(pd.astype(BF), vals(diag))
        if n:
            po = jnp.exp2((so - m) * SCALE)
            l = l + jnp.sum(po, axis=1, keepdims=True)
            o = o + nn(po.astype(BF), vals(pl.ds(lo, n)))
        lse = m * SCALE + jnp.log2(l)
        lse_ref[diag, pl.ds(h, 1)] = lse
        return o / l

    def blocks(b):
        return range(b * TOK // QB // 2, (b + 1) * TOK // QB // 2)

    def own(h, b):
        for i in blocks(b):
            tok = pl.ds(i * QB, QB)
            o_own[tok, lanes(h)] = attend(
                aq_v[tok, lanes(h)], lambda r: ak_v[r, lanes(h)], lambda r: av_v[r, lanes(h)],
                i, True, lse_own, h,
            )

    def serve(h, b):
        if h < SERVED:
            q_copy(h, b).wait_recv()
            for i in blocks(b):
                tok = pl.ds(i * QB, QB)
                o_send[h, tok, :] = attend(
                    qn[h, tok, :], lambda r: ak_v[r, lanes(h)], lambda r: av_v[r, lanes(h)],
                    i, False, lse_nb, h,
                ).astype(BF)
            o_copy(h, b).start()
        else:
            n = h - SERVED
            for i in blocks(b):
                tok = pl.ds(i * QB, QB)
                o_recv[h, tok, :] = attend(
                    aq_v[tok, lanes(h)], lambda r: kn[n, r, :], lambda r: vn[n, r, :],
                    i, False, lse_kv, h,
                ).astype(BF)

    lse_own[...] = jnp.zeros_like(lse_own)
    lse_nb[...] = jnp.zeros_like(lse_nb)

    def send_lse():
        for i in range(TOK // HD):
            lse_send[:, pl.ds(i * HD, HD)] = lse_nb[pl.ds(i * HD, HD), :].T[0:8, :]
        lse_copy().start()

    def merge():
        for h in range(SERVED):
            for b in range(2):
                o_copy(h, b).wait_recv()
        lse_copy().wait_recv()
        for i in range(TOK // HD):
            tok = pl.ds(i * HD, HD)
            theirs = jnp.concatenate([lse_recv[:, tok], jnp.zeros((HD - 8, HD), F32)], axis=0).T
            for h in range(HEADS):
                t = theirs[:, h : h + 1] if h < SERVED else lse_kv[tok, h : h + 1]
                t = jnp.where(seq == 0, NEG, t)
                k = 1.0 / (1.0 + jnp.exp2(t - lse_own[tok, h : h + 1]))
                o_own[tok, lanes(h)] = (
                    o_own[tok, lanes(h)] * k + o_recv[h, tok, :].astype(F32) * (1.0 - k)
                )

    squares = []

    def apply(c, first, last):
        base, width, *_ = sizes(c)
        u = nstack[pl.ds(base + 2 * width, width), :].astype(F32)
        squares.append(jnp.sum(u * u, axis=0, keepdims=True))
        if last:
            old = w2_v[...]
            factor = jnp.sqrt(jnp.sum(old * old, axis=0, keepdims=True)) / jnp.sqrt(
                sum(squares) + EPS
            )

        def tokens(i, _):
            tok = pl.ds(pl.multiple_of(i * QB, QB), QB)
            q = fq_v[tok, :]
            pg = nt(q, nstack[pl.ds(base, width), :])
            pu = nt(q, nstack[pl.ds(base + width, width), :])
            hid = (pg * jax.nn.sigmoid(pg) * pu).astype(BF)
            o = nn(hid, nstack[pl.ds(base + 2 * width, width), :])
            if not first:
                o = acc[tok, :] + o
            if last:
                out[tok, :] = (o_own[tok, :] + o * factor).astype(BF)
            else:
                acc[tok, :] = o
            return 0

        lax.fori_loop(0, TOK // QB, tokens, 0)

    waited = set()

    def loaded(*names):
        for i in names:
            if i not in waited:
                waited.add(i)
                loads[i].wait()

    applied = [0]
    merged = [False]
    left = set((h, b) for h in range(SERVED) for b in range(2))
    for token in ORDER:
        kind, first = token[0], int(token[1:2] or 0)
        b = int(token[2]) if len(token) > 2 else 0
        if kind == "q":
            q_copy(first, b).start()
        elif kind == "v":
            for cp in kv_copies(first, b):
                cp.start()
        elif kind == "o":
            loaded(6, 7, 8)
            own(first, b)
        elif kind == "s":
            loaded(6, 7, 8)
            if first >= SERVED:
                for part_ in (1, 0):
                    if part_ >= b and (first, part_) not in waited:
                        waited.add((first, part_))
                        for cp in kv_copies(first, part_):
                            cp.wait_recv()
            serve(first, b)
            if first < SERVED:
                left.discard((first, b))
                if not left:
                    send_lse()
        elif kind == "G":
            loaded(*range(6))
            prepare(first)
            grads(first)
            rs1_start(first)
        elif kind == "m":
            rs1_mid(first)
        elif kind == "e":
            rs1_end(first)
        elif kind == "r":
            rs2_end(first)
        elif kind == "a":
            ag2_end(first)
        elif kind == "f":
            ag1_fwd(first)
        elif kind == "M":
            merge()
        elif kind == "P":
            loaded(9)
            ag1_end(first)
            applied[0] += 1
            apply(first, applied[0] == 1, applied[0] == len(CHUNKS))

    for h in range(HEADS):
        for b in range(2):
            if h < SERVED:
                q_copy(h, b).wait_send()
                o_copy(h, b).wait_send()
            else:
                for cp in kv_copies(h, b):
                    cp.wait_send()
    lse_copy().wait_send()
    for c in range(len(CHUNKS)):
        for cp in (*rs1_copies(c), *rs2_copies(c), *ag2_copies(c), *ag1_copies(c)):
            cp.wait_send()


def shards(attn_q, attn_k, attn_v, fast_q, fast_k, fast_v, rates, fast_gate, fast_up, fast_down):
    rows = TOK
    act = pltpu.VMEM((rows, FWD), BF)
    weight = pltpu.VMEM((FWD, FWD), F32)
    n = len(CHUNKS)
    half = [3 * w // 8 for _, w, _ in CHUNKS]
    share = max(up16(3 * w // 16) for _, w, _ in CHUNKS)
    scratch = [
        act, act, act, act, act, act, pltpu.VMEM((1, rows), F32), weight, weight, weight,
        pltpu.VMEM((3 * FWD, FWD), F32),
        pltpu.VMEM((3 * FWD, FWD), BF),
        pltpu.VMEM((3 * FWD, FWD), F32),
        pltpu.VMEM((3 * FWD, FWD), BF),
        *[pltpu.VMEM((6, h, FWD), BF) for h in half],
        *[pltpu.VMEM((2, h, FWD), BF) for h in half],
        pltpu.VMEM((2 * max(half), FWD), F32),
        pltpu.VMEM((n, 3, share, FWD), BF),
        pltpu.VMEM((n, 3, share, FWD), BF),
        pltpu.VMEM((n, share, FWD), BF),
        pltpu.VMEM((n, 3, share, FWD), BF),
        pltpu.VMEM((3 * FWD, FWD), BF),
        pltpu.VMEM((SERVED, rows, HD), BF),
        pltpu.VMEM((KV_HEADS, rows, HD), BF),
        pltpu.VMEM((KV_HEADS, rows, HD), BF),
        pltpu.VMEM((SERVED, rows, HD), BF),
        pltpu.VMEM((HEADS, rows, HD), BF),
        pltpu.VMEM((rows, FWD), F32),
        pltpu.VMEM((rows, HD), F32),
        pltpu.VMEM((rows, HD), F32),
        pltpu.VMEM((rows, HD), F32),
        pltpu.VMEM((8, rows), F32),
        pltpu.VMEM((8, rows), F32),
        pltpu.VMEM((rows, FWD), F32),
        pltpu.SemaphoreType.DMA((10,)),
        *[pltpu.SemaphoreType.DMA((SERVED, 2))] * 4,
        *[pltpu.SemaphoreType.DMA((KV_HEADS, 2, 2))] * 2,
        pltpu.SemaphoreType.DMA((1,)),
        pltpu.SemaphoreType.DMA((1,)),
        pltpu.SemaphoreType.DMA((n, 18)),
        pltpu.SemaphoreType.DMA((n, 18)),
    ]
    square = fast_gate.reshape(FWD, FWD), fast_up.reshape(FWD, FWD), fast_down.reshape(FWD, FWD)
    return pl.pallas_call(
        kernel,
        out_shape=jax.ShapeDtypeStruct((rows, FWD), BF),
        in_specs=[pl.BlockSpec(memory_space=pl.ANY)] * 10,
        out_specs=pl.BlockSpec(memory_space=pltpu.VMEM),
        scratch_shapes=scratch,
        compiler_params=pltpu.CompilerParams(
            collective_id=0, has_side_effects=True, vmem_limit_bytes=60 << 20
        ),
    )(attn_q, attn_k, attn_v, fast_q, fast_k, fast_v, rates.reshape(1, rows), *square)


def solution(mesh):
    placed = (P("seq", "head"),) * 7 + (P("head", None, None),) * 3
    return jax.shard_map(
        shards, mesh=mesh, in_specs=placed, out_specs=P("seq", "head"), check_vma=False
    )
```

```python
import math

import jax
import jax.numpy as jnp
from jax import lax
from jax.experimental import pallas as pl
from jax.experimental.pallas import tpu as pltpu
from jax.sharding import PartitionSpec as P

HD = 128
FWD = 640
TOK = 1024
HEADS = 5
QB = 256
TB = 512
AB = 512
PIECES = 1
EPS = 1e-06
MESH = pl.DeviceIdType.MESH
SCALE = math.log2(math.e) / math.sqrt(HD)
NEG = -1e30
BF = jnp.bfloat16
F32 = jnp.float32

CHUNKS = ((0, 256, "x"), (256, 256, "y"), (512, 128, "x"))


class Remote:
    def __init__(self, src, dst, send_sem, recv_sem, device):
        self.parts = src, dst, send_sem, recv_sem
        self.device = device

    def copy(self):
        return pltpu.make_async_remote_copy(
            *self.parts, device_id=self.device, device_id_type=MESH
        )

    def start(self):
        self.copy().start()

    def wait_recv(self):
        self.copy().wait_recv()

    def wait_send(self):
        self.copy().wait_send()


ORDER = (
    "q00", "v40", "q31", "q30", "v41", "q20", "G0", "G1", "s31", "q21", "G2", "m0",
    "m1", "q01", "o41", "s00", "o11", "m2", "o40", "q11", "s30", "o20", "e1", "o01",
    "e2", "e0", "o30", "s01", "r2", "r1", "r0", "s11", "o21", "q10", "a2", "a1",
    "s21", "a0", "s40", "o31", "f2", "f1", "s10", "o00", "f0", "s41", "s20", "P2",
    "o10", "P1", "M", "P0",
)
KV_HEADS = 1
SHIFT = 1
SERVED = HEADS - KV_HEADS


def up16(n):
    return (n + 15) // 16 * 16


def nt(a, b):
    return lax.dot_general(a, b, (((1,), (1,)), ((), ())), preferred_element_type=F32)


def nn(a, b):
    return lax.dot_general(a, b, (((1,), (0,)), ((), ())), preferred_element_type=F32)


def kernel(
    aq, ak, av, fq, fk, fv, rt, w1, w3, w2, out,
    aq_v, ak_v, av_v, fq_v, fk_v, fv_v, rt_v, w1_v, w3_v, w2_v,
    mstack, mbf, gsum, gbf, rx0, rx1, rx2, fb0, fb1, fb2, part, share_out, share_in,
    new_out, new_in, nstack, qn, kn, vn, o_send, o_recv, o_own, lse_own, lse_nb, lse_kv, lse_send, lse_recv,
    acc, side, res, ld_sem, st_sem, q_ss, q_rs, o_ss, o_rs, k_ss, k_rs, l_ss, l_rs, c_ss, c_rs,
):
    seq = lax.axis_index("seq")
    head = lax.axis_index("head")
    cx = seq // 4
    cy = lax.rem(seq, 4)
    rx = (rx0, rx1, rx2)
    fb = (fb0, fb1, fb2)

    def at(axis, d):
        if axis == "x":
            return (lax.rem(cx + d + 4, 4) * 4 + cy, head)
        return (cx * 4 + lax.rem(cy + d + 4, 4), head)

    def coord(axis, d=0):
        return lax.rem((cx if axis == "x" else cy) + d + 4, 4)

    before = (lax.rem(seq + 15, 16), head)
    after = (lax.rem(seq + 1, 16), head)

    loads = [
        pltpu.make_async_copy(src, dst, ld_sem.at[i])
        for i, (src, dst) in enumerate(
            (
                (fk, fk_v), (w1, w1_v), (w3, w3_v), (w2, w2_v), (fv, fv_v), (rt, rt_v),
                (aq, aq_v), (ak, ak_v), (av, av_v), (fq, fq_v),
            )
        )
    ]
    for c in loads[:6]:
        c.start()

    barrier = pltpu.get_barrier_semaphore()
    peers = [at(a, d) for a in ("x", "y") for d in (1, -1, 2)] + [before, after]
    for p in peers:
        pl.semaphore_signal(barrier, inc=1, device_id=p, device_id_type=MESH)
    pl.semaphore_wait(barrier, len(peers))

    def lanes(h):
        if isinstance(h, int):
            return pl.ds(h * HD, HD)
        return pl.ds(pl.multiple_of(h * HD, HD), HD)

    def half(b):
        return pl.ds(b * TOK // 2, TOK // 2)

    def q_copy(h, b):
        return Remote(
            aq.at[half(b), lanes(h)], qn.at[h, half(b)], q_ss.at[h, b], q_rs.at[h, b], before
        )

    def o_copy(h, b):
        return Remote(
            o_send.at[h, half(b)], o_recv.at[h, half(b)], o_ss.at[h, b], o_rs.at[h, b], after
        )

    def kv_copies(h, b):
        n = h - SERVED
        return [
            Remote(
                src.at[half(b), lanes(h)], dst.at[n, half(b)],
                k_ss.at[n, b, i], k_rs.at[n, b, i], after,
            )
            for i, (src, dst) in enumerate(((ak, kn), (av, vn)))
        ]

    def lse_copy():
        return Remote(lse_send, lse_recv, l_ss.at[0], l_rs.at[0], after)

    def sizes(c):
        first, width, axis = CHUNKS[c]
        rows = 3 * width
        return 3 * first, width, rows, rows // 4, rows // 8, rows // 16, axis, "y" if axis == "x" else "x"

    def rows_of(base, index, n):
        return pl.ds(pl.multiple_of(base + index * n, 8 if n % 16 else 16), n)

    def way(a, k):
        sign = 1 - 2 * k
        if a == "x":
            sign = jnp.where(cy == 0, SHIFT, jnp.where(cy == 3, -SHIFT, sign)) if SHIFT else sign
        return sign

    def wayg(a, k):
        return -1 if a == "y" else way(a, k)

    def rs1_copies(c):
        base, _, _, p, hf, _, a, _ = sizes(c)
        op = coord(a, 2)
        ss, rs, r = c_ss.at[c], c_rs.at[c], rx[c]
        copies = []
        for k in range(2):
            to = way(a, k)
            copies.append(
                Remote(gbf.at[rows_of(base, op * 2 + k, hf)], r.at[k], ss.at[k], rs.at[k], at(a, to))
            )
        for k in (1, 0):
            to = -way(a, k)
            copies.append(
                Remote(
                    gbf.at[rows_of(base, coord(a, to) * 2 + k, hf)], r.at[2 + k],
                    ss.at[2 + k], rs.at[2 + k], at(a, to),
                )
            )
        for k in range(2):
            copies.append(
                Remote(fb[c].at[k], r.at[4 + k], ss.at[4 + k], rs.at[4 + k], at(a, way(a, k)))
            )
        return copies

    def rs1_start(c):
        for cp in rs1_copies(c)[:4]:
            cp.start()

    def rs1_mid(c):
        base, _, _, _, hf, _, a, _ = sizes(c)
        cps = rs1_copies(c)
        for k in range(2):
            cps[k].wait_recv()
            rows = rows_of(base, coord(a, way(a, k)) * 2 + k, hf)
            fb[c][k] = (gsum[rows, :] + rx[c][k].astype(F32)).astype(BF)
            cps[4 + k].start()

    def rs2_copies(c):
        _, _, _, _, _, s, _, b = sizes(c)
        s = up16(s)
        ss, rs = c_ss.at[c], c_rs.at[c]
        return [
            Remote(
                share_out.at[c, d - 1, pl.ds(0, s)], share_in.at[c, d - 1, pl.ds(0, s)],
                ss.at[5 + d], rs.at[5 + d], at(b, d),
            )
            for d in (1, 2, 3)
        ]

    def rs1_end(c):
        base, _, _, p, hf, s, a, b = sizes(c)
        cps = rs1_copies(c)
        for i in (2, 3, 4, 5):
            cps[i].wait_recv()
        r = rx[c]
        mine = coord(a)
        for k in range(2):
            part[pl.ds(k * hf, hf), :] = (
                gsum[rows_of(base, mine * 2 + k, hf), :]
                + r[2 + k].astype(F32)
                + r[4 + k].astype(F32)
            )
        for d, cp in zip((1, 2, 3), rs2_copies(c)):
            share_out[c, d - 1, pl.ds(0, s), :] = part[rows_of(0, coord(b, d), s), :].astype(BF)
            cp.start()
        gsum[pl.ds(base, s), :] = part[rows_of(0, coord(b), s), :]

    def ag2_copies(c):
        _, _, _, _, _, s, _, b = sizes(c)
        s = up16(s)
        ss, rs = c_ss.at[c], c_rs.at[c]
        return [
            Remote(
                new_out.at[c, pl.ds(0, s)], new_in.at[c, d - 1, pl.ds(0, s)],
                ss.at[8 + d], rs.at[8 + d], at(b, d),
            )
            for d in (1, 2, 3)
        ]

    def rs2_end(c):
        base, width, _, p, _, s, a, b = sizes(c)
        for cp in rs2_copies(c):
            cp.wait_recv()
        total = gsum[pl.ds(base, s), :]
        for d in range(3):
            total = total + share_in[c, d, pl.ds(0, s), :].astype(F32)
        start = coord(a) * p + coord(b) * s
        old = mstack[pl.ds(pl.multiple_of(base + start, 8), s), :]
        new = old - total
        old_norm = jnp.sqrt(jnp.sum(old * old, axis=1, keepdims=True))
        new_norm = jnp.sqrt(jnp.sum(new * new, axis=1, keepdims=True) + EPS)
        row = start + lax.broadcasted_iota(jnp.int32, (s, 1), 0)
        factor = jnp.where(row < 2 * width, old_norm / new_norm, 1.0)
        new_out[c, pl.ds(0, s), :] = (new * factor).astype(BF)
        for cp in ag2_copies(c):
            cp.start()

    def ag1_copies(c):
        base, _, _, p, hf, _, a, _ = sizes(c)
        ss, rs = c_ss.at[c], c_rs.at[c]
        me = coord(a)

        def same(index, k, i, to):
            rows = rows_of(base, index * 2 + k, hf)
            return Remote(nstack.at[rows], nstack.at[rows], ss.at[i], rs.at[i], at(a, to))

        return (
            *[same(me, k, 12 + k, wayg(a, k)) for k in range(2)],
            *[same(me, k, 14 + k, -wayg(a, k)) for k in (1, 0)],
            *[same(coord(a, -wayg(a, k)), k, 16 + k, wayg(a, k)) for k in range(2)],
        )

    def ag2_end(c):
        base, _, _, p, _, s, a, b = sizes(c)
        for cp in ag2_copies(c):
            cp.wait_recv()
        part[rows_of(0, coord(b), s), :] = new_out[c, pl.ds(0, s), :].astype(F32)
        for d in (1, 2, 3):
            part[rows_of(0, coord(b, -d), s), :] = new_in[c, d - 1, pl.ds(0, s), :].astype(F32)
        nstack[rows_of(base, coord(a), p), :] = part[pl.ds(0, p), :].astype(BF)
        for cp in ag1_copies(c)[:4]:
            cp.start()

    def ag1_fwd(c):
        cps = ag1_copies(c)
        cps[0].wait_recv()
        cps[4].start()
        cps[1].wait_recv()
        cps[5].start()

    def ag1_end(c):
        cps = ag1_copies(c)
        for cp in cps[2:]:
            cp.wait_recv()

    def prepare(c):
        first, width, _ = CHUNKS[c]
        base = 3 * first
        for k in range(width // 128):
            cols = pl.ds(first + k * 128, 128)
            for n, ref in ((0, w1_v), (1, w3_v)):
                t = ref[:, cols].T
                mstack[pl.ds(base + n * width + k * 128, 128), :] = t
                mbf[pl.ds(base + n * width + k * 128, 128), :] = t.astype(BF)
        t = w2_v[pl.ds(first, width), :]
        mstack[pl.ds(base + 2 * width, width), :] = t
        mbf[pl.ds(base + 2 * width, width), :] = t.astype(BF)

    def grads(c):
        first, width, _ = CHUNKS[c]
        base = 3 * first
        rows = [pl.ds(base + n * width, width) for n in range(3)]

        for i in range(TOK // TB):
            tok = pl.ds(i * TB, TB)
            key = fk_v[tok, :]
            val = fv_v[tok, :]
            rate = -rt_v[:, tok]
            pre = nt(mbf[pl.ds(base, 2 * width), :], key)
            pg, pu = pre[:width], pre[width:]
            hg = nt(mbf[rows[2], :], val) * rate
            sg = jax.nn.sigmoid(pg)
            act = pg * sg
            side[pl.ds(0, width), :] = (hg * pu * sg * (1.0 + pg * (1.0 - sg))).astype(BF)
            side[pl.ds(width, width), :] = (hg * act).astype(BF)
            side[pl.ds(2 * width, width), :] = (act * pu * rate).astype(BF)
            both = pl.ds(base, 2 * width)
            in_part = nn(side[pl.ds(0, 2 * width), :], key)
            out_part = nn(side[pl.ds(2 * width, width), :], val)
            if i:
                in_part = gsum[both, :] + in_part
                out_part = gsum[rows[2], :] + out_part
            gsum[both, :] = in_part
            gsum[rows[2], :] = out_part
            if i == TOK // TB - 1:
                gbf[both, :] = in_part.astype(BF)
                gbf[rows[2], :] = out_part.astype(BF)

    row_i = lax.broadcasted_iota(jnp.int32, (QB, QB), 0)
    col_i = lax.broadcasted_iota(jnp.int32, (QB, QB), 1)

    def attend(q, keys, vals, i, own, lse_ref, h):
        diag = pl.ds(i * QB, QB)
        if own:
            lo, n = 0, i * QB
        else:
            lo, n = (i + 1) * QB, TOK - (i + 1) * QB
        sd = nt(q, keys(diag))
        sd = jnp.where((col_i <= row_i) if own else (col_i >= row_i), sd, NEG)
        m = jnp.max(sd, axis=1, keepdims=True)
        if n:
            so = nt(q, keys(pl.ds(lo, n)))
            m = jnp.maximum(m, jnp.max(so, axis=1, keepdims=True))
        pd = jnp.exp2((sd - m) * SCALE)
        l = jnp.sum(pd, axis=1, keepdims=True)
        o = nn(pd.astype(BF), vals(diag))
        if n:
            po = jnp.exp2((so - m) * SCALE)
            l = l + jnp.sum(po, axis=1, keepdims=True)
            o = o + nn(po.astype(BF), vals(pl.ds(lo, n)))
        lse = m * SCALE + jnp.log2(l)
        lse_ref[diag, pl.ds(h, 1)] = lse
        return o / l

    def blocks(b):
        return range(b * TOK // QB // 2, (b + 1) * TOK // QB // 2)

    def own(h, b):
        for i in blocks(b):
            tok = pl.ds(i * QB, QB)
            o_own[tok, lanes(h)] = attend(
                aq_v[tok, lanes(h)], lambda r: ak_v[r, lanes(h)], lambda r: av_v[r, lanes(h)],
                i, True, lse_own, h,
            )

    def serve(h, b):
        if h < SERVED:
            q_copy(h, b).wait_recv()
            for i in blocks(b):
                tok = pl.ds(i * QB, QB)
                o_send[h, tok, :] = attend(
                    qn[h, tok, :], lambda r: ak_v[r, lanes(h)], lambda r: av_v[r, lanes(h)],
                    i, False, lse_nb, h,
                ).astype(BF)
            o_copy(h, b).start()
        else:
            n = h - SERVED
            for i in blocks(b):
                tok = pl.ds(i * QB, QB)
                o_recv[h, tok, :] = attend(
                    aq_v[tok, lanes(h)], lambda r: kn[n, r, :], lambda r: vn[n, r, :],
                    i, False, lse_kv, h,
                ).astype(BF)

    lse_own[...] = jnp.zeros_like(lse_own)
    lse_nb[...] = jnp.zeros_like(lse_nb)

    def send_lse():
        for i in range(TOK // HD):
            lse_send[:, pl.ds(i * HD, HD)] = lse_nb[pl.ds(i * HD, HD), :].T[0:8, :]
        lse_copy().start()

    def merge():
        for h in range(SERVED):
            for b in range(2):
                o_copy(h, b).wait_recv()
        lse_copy().wait_recv()
        for i in range(TOK // HD):
            tok = pl.ds(i * HD, HD)
            theirs = jnp.concatenate([lse_recv[:, tok], jnp.zeros((HD - 8, HD), F32)], axis=0).T
            for h in range(HEADS):
                t = theirs[:, h : h + 1] if h < SERVED else lse_kv[tok, h : h + 1]
                t = jnp.where(seq == 0, NEG, t)
                k = 1.0 / (1.0 + jnp.exp2(t - lse_own[tok, h : h + 1]))
                o_own[tok, lanes(h)] = (
                    o_own[tok, lanes(h)] * k + o_recv[h, tok, :].astype(F32) * (1.0 - k)
                )

    squares = []
    stores = []

    def apply(c, first, last):
        base, width, *_ = sizes(c)
        u = nstack[pl.ds(base + 2 * width, width), :].astype(F32)
        squares.append(jnp.sum(u * u, axis=0, keepdims=True))
        if last:
            old = w2_v[...]
            factor = jnp.sqrt(jnp.sum(old * old, axis=0, keepdims=True)) / jnp.sqrt(
                sum(squares) + EPS
            )

        def tokens(i, _):
            tok = pl.ds(i * AB if last else pl.multiple_of(i * AB, AB), AB)
            q = fq_v[tok, :]
            pre = nt(q, nstack[pl.ds(base, 2 * width), :])
            pg, pu = pre[:, :width], pre[:, width:]
            hid = (pg * jax.nn.sigmoid(pg) * pu).astype(BF)
            o = nn(hid, nstack[pl.ds(base + 2 * width, width), :])
            if not first:
                o = acc[tok, :] + o
            if last:
                res[tok, :] = (o_own[tok, :] + o * factor).astype(BF)
            else:
                acc[tok, :] = o
            return 0

        if not last:
            lax.fori_loop(0, TOK // AB, tokens, 0)
        else:
            for i in range(TOK // AB):
                tokens(i, 0)
                stores.append(
                    pltpu.make_async_copy(
                        res.at[pl.ds(i * AB, AB)], out.at[pl.ds(i * AB, AB)], st_sem.at[i]
                    )
                )
                stores[-1].start()

    waited = set()

    def loaded(*names):
        for i in names:
            if i not in waited:
                waited.add(i)
                loads[i].wait()

    applied = [0]
    grown = []
    merged = [False]
    left = set((h, b) for h in range(SERVED) for b in range(2))
    for token in ORDER:
        kind, first = token[0], int(token[1:2] or 0)
        b = int(token[2]) if len(token) > 2 else 0
        if kind == "q":
            q_copy(first, b).start()
        elif kind == "v":
            for cp in kv_copies(first, b):
                cp.start()
        elif kind == "o":
            loaded(6, 7, 8)
            own(first, b)
        elif kind == "s":
            loaded(6, 7, 8)
            if first >= SERVED:
                for part_ in (1, 0):
                    if part_ >= b and (first, part_) not in waited:
                        waited.add((first, part_))
                        for cp in kv_copies(first, part_):
                            cp.wait_recv()
            serve(first, b)
            if first < SERVED:
                left.discard((first, b))
                if not left:
                    send_lse()
        elif kind == "G":
            loaded(*range(6))
            if not grown:
                for cp in loads[6:]:
                    cp.start()
            grown.append(first)
            prepare(first)
            grads(first)
            rs1_start(first)
        elif kind == "m":
            rs1_mid(first)
        elif kind == "e":
            rs1_end(first)
        elif kind == "r":
            rs2_end(first)
        elif kind == "a":
            ag2_end(first)
        elif kind == "f":
            ag1_fwd(first)
        elif kind == "M":
            merge()
        elif kind == "P":
            loaded(9)
            ag1_end(first)
            applied[0] += 1
            apply(first, applied[0] == 1, applied[0] == len(CHUNKS))

    for cp in stores:
        cp.wait()
    for h in range(HEADS):
        for b in range(2):
            if h < SERVED:
                q_copy(h, b).wait_send()
                o_copy(h, b).wait_send()
            else:
                for cp in kv_copies(h, b):
                    cp.wait_send()
    lse_copy().wait_send()
    for c in range(len(CHUNKS)):
        for cp in (*rs1_copies(c), *rs2_copies(c), *ag2_copies(c), *ag1_copies(c)):
            cp.wait_send()


def hand_on(src, dst):
    dst[...] = src[...]


def shards(attn_q, attn_k, attn_v, fast_q, fast_k, fast_v, rates, fast_gate, fast_up, fast_down):
    rows = TOK
    act = pltpu.VMEM((rows, FWD), BF)
    weight = pltpu.VMEM((FWD, FWD), F32)
    n = len(CHUNKS)
    half = [3 * w // 8 for _, w, _ in CHUNKS]
    share = max(up16(3 * w // 16) for _, w, _ in CHUNKS)
    scratch = [
        act, act, act, act, act, act, pltpu.VMEM((1, rows), F32), weight, weight, weight,
        pltpu.VMEM((3 * FWD, FWD), F32),
        pltpu.VMEM((3 * FWD, FWD), BF),
        pltpu.VMEM((3 * FWD, FWD), F32),
        pltpu.VMEM((3 * FWD, FWD), BF),
        *[pltpu.VMEM((6, h, FWD), BF) for h in half],
        *[pltpu.VMEM((2, h, FWD), BF) for h in half],
        pltpu.VMEM((2 * max(half), FWD), F32),
        pltpu.VMEM((n, 3, share, FWD), BF),
        pltpu.VMEM((n, 3, share, FWD), BF),
        pltpu.VMEM((n, share, FWD), BF),
        pltpu.VMEM((n, 3, share, FWD), BF),
        pltpu.VMEM((3 * FWD, FWD), BF),
        pltpu.VMEM((SERVED, rows, HD), BF),
        pltpu.VMEM((KV_HEADS, rows, HD), BF),
        pltpu.VMEM((KV_HEADS, rows, HD), BF),
        pltpu.VMEM((SERVED, rows, HD), BF),
        pltpu.VMEM((HEADS, rows, HD), BF),
        pltpu.VMEM((rows, FWD), F32),
        pltpu.VMEM((rows, HD), F32),
        pltpu.VMEM((rows, HD), F32),
        pltpu.VMEM((rows, HD), F32),
        pltpu.VMEM((8, rows), F32),
        pltpu.VMEM((8, rows), F32),
        pltpu.VMEM((rows, FWD), F32),
        pltpu.VMEM((3 * 256, TB), BF),
        act,
        pltpu.SemaphoreType.DMA((10,)),
        pltpu.SemaphoreType.DMA((TOK // AB,)),
        *[pltpu.SemaphoreType.DMA((SERVED, 2))] * 4,
        *[pltpu.SemaphoreType.DMA((KV_HEADS, 2, 2))] * 2,
        pltpu.SemaphoreType.DMA((1,)),
        pltpu.SemaphoreType.DMA((1,)),
        pltpu.SemaphoreType.DMA((n, 18)),
        pltpu.SemaphoreType.DMA((n, 18)),
    ]
    square = fast_gate.reshape(FWD, FWD), fast_up.reshape(FWD, FWD), fast_down.reshape(FWD, FWD)
    out = pl.pallas_call(
        kernel,
        out_shape=jax.ShapeDtypeStruct((rows, FWD), BF),
        in_specs=[pl.BlockSpec(memory_space=pl.ANY)] * 10,
        out_specs=pl.BlockSpec(memory_space=pl.ANY),
        scratch_shapes=scratch,
        compiler_params=pltpu.CompilerParams(
            collective_id=0, has_side_effects=True, vmem_limit_bytes=60 << 20
        ),
    )(attn_q, attn_k, attn_v, fast_q, fast_k, fast_v, rates.reshape(1, rows), *square)
    block = pl.BlockSpec((rows // PIECES, FWD), lambda i: (i, 0))
    return pl.pallas_call(
        hand_on,
        grid=(PIECES,),
        out_shape=jax.ShapeDtypeStruct((rows, FWD), BF),
        in_specs=[block],
        out_specs=block,
    )(out)


def solution(mesh):
    placed = (P("seq", "head"),) * 7 + (P("head", None, None),) * 3
    return jax.shard_map(
        shards, mesh=mesh, in_specs=placed, out_specs=P("seq", "head"), check_vma=False
    )
```

```python
import math

import jax
import jax.numpy as jnp
from jax import lax
from jax.experimental import pallas as pl
from jax.experimental.pallas import tpu as pltpu
from jax.sharding import PartitionSpec as P

HD = 128
FWD = 640
TOK = 1024
HEADS = 5
QB = 256
TB = 512
AB = 512
PIECES = 2
EPS = 1e-06
MESH = pl.DeviceIdType.MESH
SCALE = math.log2(math.e) / math.sqrt(HD)
NEG = -1e30
BF = jnp.bfloat16
F32 = jnp.float32

CHUNKS = ((0, 256, "x"), (256, 256, "y"), (512, 128, "x"))


class Remote:
    def __init__(self, src, dst, send_sem, recv_sem, device):
        self.parts = src, dst, send_sem, recv_sem
        self.device = device

    def copy(self):
        return pltpu.make_async_remote_copy(
            *self.parts, device_id=self.device, device_id_type=MESH
        )

    def start(self):
        self.copy().start()

    def wait_recv(self):
        self.copy().wait_recv()

    def wait_send(self):
        self.copy().wait_send()


ORDER = (
    "q00", "v40", "q31", "q30", "v41", "q20", "G0", "G1", "s31", "q21", "G2", "m0",
    "m1", "q01", "o41", "s00", "o11", "m2", "o40", "s30", "o20", "e1", "q11", "o01",
    "e2", "e0", "o30", "s01", "r2", "r1", "r0", "s11", "o21", "q10", "a2", "a1",
    "s21", "a0", "s20", "s40", "o31", "f2", "f1", "s10", "o00", "f0", "s41", "P2",
    "o10", "P1", "M", "P0",
)
KV_HEADS = 1
SHIFT = 1
SERVED = HEADS - KV_HEADS


def up16(n):
    return (n + 15) // 16 * 16


def nt(a, b):
    return lax.dot_general(a, b, (((1,), (1,)), ((), ())), preferred_element_type=F32)


def nn(a, b):
    return lax.dot_general(a, b, (((1,), (0,)), ((), ())), preferred_element_type=F32)


def kernel(
    aq, ak, av, fq, fk, fv, rt, w1, w3, w2, out,
    aq_v, ak_v, av_v, fq_v, fk_v, fv_v, rt_v, w1_v, w3_v, w2_v,
    mstack, mbf, gsum, gbf, rx0, rx1, rx2, fb0, fb1, fb2, part, share_out, share_in,
    new_out, new_in, nstack, qn, kn, vn, o_send, o_recv, o_own, lse_own, lse_nb, lse_kv, lse_send, lse_recv,
    acc, side, res, ld_sem, st_sem, q_ss, q_rs, o_ss, o_rs, k_ss, k_rs, l_ss, l_rs, c_ss, c_rs,
):
    seq = lax.axis_index("seq")
    head = lax.axis_index("head")
    cx = seq // 4
    cy = lax.rem(seq, 4)
    rx = (rx0, rx1, rx2)
    fb = (fb0, fb1, fb2)

    def at(axis, d):
        if axis == "x":
            return (lax.rem(cx + d + 4, 4) * 4 + cy, head)
        return (cx * 4 + lax.rem(cy + d + 4, 4), head)

    def coord(axis, d=0):
        return lax.rem((cx if axis == "x" else cy) + d + 4, 4)

    before = (lax.rem(seq + 15, 16), head)
    after = (lax.rem(seq + 1, 16), head)

    early = pl.ds(CHUNKS[0][0], CHUNKS[0][1])
    late = pl.ds(CHUNKS[0][1], FWD - CHUNKS[0][1])
    loads = [
        pltpu.make_async_copy(src, dst, ld_sem.at[i])
        for i, (src, dst) in enumerate(
            (
                (fk, fk_v), (w1.at[:, early], w1_v.at[:, early]),
                (w3.at[:, early], w3_v.at[:, early]), (w2.at[early], w2_v.at[early]),
                (fv, fv_v), (rt, rt_v),
                (aq, aq_v), (ak, ak_v), (av, av_v), (fq, fq_v),
                (w1.at[:, late], w1_v.at[:, late]),
                (w3.at[:, late], w3_v.at[:, late]), (w2.at[late], w2_v.at[late]),
            )
        )
    ]
    for c in loads[:6]:
        c.start()

    barrier = pltpu.get_barrier_semaphore()
    peers = [at(a, d) for a in ("x", "y") for d in (1, -1, 2)] + [before, after]
    for p in peers:
        pl.semaphore_signal(barrier, inc=1, device_id=p, device_id_type=MESH)
    pl.semaphore_wait(barrier, len(peers))

    def lanes(h):
        if isinstance(h, int):
            return pl.ds(h * HD, HD)
        return pl.ds(pl.multiple_of(h * HD, HD), HD)

    def half(b):
        return pl.ds(b * TOK // 2, TOK // 2)

    def q_copy(h, b):
        return Remote(
            aq.at[half(b), lanes(h)], qn.at[h, half(b)], q_ss.at[h, b], q_rs.at[h, b], before
        )

    def o_copy(h, b):
        return Remote(
            o_send.at[h, half(b)], o_recv.at[h, half(b)], o_ss.at[h, b], o_rs.at[h, b], after
        )

    def kv_copies(h, b):
        n = h - SERVED
        return [
            Remote(
                src.at[half(b), lanes(h)], dst.at[n, half(b)],
                k_ss.at[n, b, i], k_rs.at[n, b, i], after,
            )
            for i, (src, dst) in enumerate(((ak, kn), (av, vn)))
        ]

    def lse_copy():
        return Remote(lse_send, lse_recv, l_ss.at[0], l_rs.at[0], after)

    def sizes(c):
        first, width, axis = CHUNKS[c]
        rows = 3 * width
        return 3 * first, width, rows, rows // 4, rows // 8, rows // 16, axis, "y" if axis == "x" else "x"

    def rows_of(base, index, n):
        return pl.ds(pl.multiple_of(base + index * n, 8 if n % 16 else 16), n)

    def way(a, k):
        sign = 1 - 2 * k
        if a == "x":
            sign = jnp.where(cy == 0, SHIFT, jnp.where(cy == 3, -SHIFT, sign)) if SHIFT else sign
        return sign

    def wayg(a, k):
        return -1 if a == "y" else way(a, k)

    def rs1_copies(c):
        base, _, _, p, hf, _, a, _ = sizes(c)
        op = coord(a, 2)
        ss, rs, r = c_ss.at[c], c_rs.at[c], rx[c]
        copies = []
        for k in range(2):
            to = way(a, k)
            copies.append(
                Remote(gbf.at[rows_of(base, op * 2 + k, hf)], r.at[k], ss.at[k], rs.at[k], at(a, to))
            )
        for k in (1, 0):
            to = -way(a, k)
            copies.append(
                Remote(
                    gbf.at[rows_of(base, coord(a, to) * 2 + k, hf)], r.at[2 + k],
                    ss.at[2 + k], rs.at[2 + k], at(a, to),
                )
            )
        for k in range(2):
            copies.append(
                Remote(fb[c].at[k], r.at[4 + k], ss.at[4 + k], rs.at[4 + k], at(a, way(a, k)))
            )
        return copies

    def rs1_start(c):
        for cp in rs1_copies(c)[:4]:
            cp.start()

    def rs1_mid(c):
        base, _, _, _, hf, _, a, _ = sizes(c)
        cps = rs1_copies(c)
        for k in range(2):
            cps[k].wait_recv()
            rows = rows_of(base, coord(a, way(a, k)) * 2 + k, hf)
            fb[c][k] = (gsum[rows, :] + rx[c][k].astype(F32)).astype(BF)
            cps[4 + k].start()

    def rs2_copies(c):
        _, _, _, _, _, s, _, b = sizes(c)
        s = up16(s)
        ss, rs = c_ss.at[c], c_rs.at[c]
        return [
            Remote(
                share_out.at[c, d - 1, pl.ds(0, s)], share_in.at[c, d - 1, pl.ds(0, s)],
                ss.at[5 + d], rs.at[5 + d], at(b, d),
            )
            for d in (1, 2, 3)
        ]

    def rs1_end(c):
        base, _, _, p, hf, s, a, b = sizes(c)
        cps = rs1_copies(c)
        for i in (2, 3, 4, 5):
            cps[i].wait_recv()
        r = rx[c]
        mine = coord(a)
        for k in range(2):
            part[pl.ds(k * hf, hf), :] = (
                gsum[rows_of(base, mine * 2 + k, hf), :]
                + r[2 + k].astype(F32)
                + r[4 + k].astype(F32)
            )
        for d, cp in zip((1, 2, 3), rs2_copies(c)):
            share_out[c, d - 1, pl.ds(0, s), :] = part[rows_of(0, coord(b, d), s), :].astype(BF)
            cp.start()
        gsum[pl.ds(base, s), :] = part[rows_of(0, coord(b), s), :]

    def ag2_copies(c):
        _, _, _, _, _, s, _, b = sizes(c)
        s = up16(s)
        ss, rs = c_ss.at[c], c_rs.at[c]
        return [
            Remote(
                new_out.at[c, pl.ds(0, s)], new_in.at[c, d - 1, pl.ds(0, s)],
                ss.at[8 + d], rs.at[8 + d], at(b, d),
            )
            for d in (1, 2, 3)
        ]

    def rs2_end(c):
        base, width, _, p, _, s, a, b = sizes(c)
        for cp in rs2_copies(c):
            cp.wait_recv()
        total = gsum[pl.ds(base, s), :]
        for d in range(3):
            total = total + share_in[c, d, pl.ds(0, s), :].astype(F32)
        start = coord(a) * p + coord(b) * s
        old = mstack[pl.ds(pl.multiple_of(base + start, 8), s), :]
        new = old - total
        old_norm = jnp.sqrt(jnp.sum(old * old, axis=1, keepdims=True))
        new_norm = jnp.sqrt(jnp.sum(new * new, axis=1, keepdims=True) + EPS)
        row = start + lax.broadcasted_iota(jnp.int32, (s, 1), 0)
        factor = jnp.where(row < 2 * width, old_norm / new_norm, 1.0)
        new_out[c, pl.ds(0, s), :] = (new * factor).astype(BF)
        for cp in ag2_copies(c):
            cp.start()

    def ag1_copies(c):
        base, _, _, p, hf, _, a, _ = sizes(c)
        ss, rs = c_ss.at[c], c_rs.at[c]
        me = coord(a)

        def same(index, k, i, to):
            rows = rows_of(base, index * 2 + k, hf)
            return Remote(nstack.at[rows], nstack.at[rows], ss.at[i], rs.at[i], at(a, to))

        return (
            *[same(me, k, 12 + k, wayg(a, k)) for k in range(2)],
            *[same(me, k, 14 + k, -wayg(a, k)) for k in (1, 0)],
            *[same(coord(a, -wayg(a, k)), k, 16 + k, wayg(a, k)) for k in range(2)],
        )

    def ag2_end(c):
        base, _, _, p, _, s, a, b = sizes(c)
        for cp in ag2_copies(c):
            cp.wait_recv()
        part[rows_of(0, coord(b), s), :] = new_out[c, pl.ds(0, s), :].astype(F32)
        for d in (1, 2, 3):
            part[rows_of(0, coord(b, -d), s), :] = new_in[c, d - 1, pl.ds(0, s), :].astype(F32)
        nstack[rows_of(base, coord(a), p), :] = part[pl.ds(0, p), :].astype(BF)
        for cp in ag1_copies(c)[:4]:
            cp.start()

    def ag1_fwd(c):
        cps = ag1_copies(c)
        cps[0].wait_recv()
        cps[4].start()
        cps[1].wait_recv()
        cps[5].start()

    def ag1_end(c):
        cps = ag1_copies(c)
        for cp in cps[2:]:
            cp.wait_recv()

    def prepare(c):
        first, width, _ = CHUNKS[c]
        base = 3 * first
        for k in range(width // 128):
            cols = pl.ds(first + k * 128, 128)
            for n, ref in ((0, w1_v), (1, w3_v)):
                t = ref[:, cols].T
                mstack[pl.ds(base + n * width + k * 128, 128), :] = t
                mbf[pl.ds(base + n * width + k * 128, 128), :] = t.astype(BF)
        t = w2_v[pl.ds(first, width), :]
        mstack[pl.ds(base + 2 * width, width), :] = t
        mbf[pl.ds(base + 2 * width, width), :] = t.astype(BF)

    def grads(c):
        first, width, _ = CHUNKS[c]
        base = 3 * first
        rows = [pl.ds(base + n * width, width) for n in range(3)]

        for i in range(TOK // TB):
            tok = pl.ds(i * TB, TB)
            key = fk_v[tok, :]
            val = fv_v[tok, :]
            rate = -rt_v[:, tok]
            pre = nt(mbf[pl.ds(base, 2 * width), :], key)
            pg, pu = pre[:width], pre[width:]
            hg = nt(mbf[rows[2], :], val) * rate
            sg = jax.nn.sigmoid(pg)
            act = pg * sg
            side[pl.ds(0, width), :] = (hg * pu * sg * (1.0 + pg * (1.0 - sg))).astype(BF)
            side[pl.ds(width, width), :] = (hg * act).astype(BF)
            side[pl.ds(2 * width, width), :] = (act * pu * rate).astype(BF)
            both = pl.ds(base, 2 * width)
            in_part = nn(side[pl.ds(0, 2 * width), :], key)
            out_part = nn(side[pl.ds(2 * width, width), :], val)
            if i:
                in_part = gsum[both, :] + in_part
                out_part = gsum[rows[2], :] + out_part
            gsum[both, :] = in_part
            gsum[rows[2], :] = out_part
            if i == TOK // TB - 1:
                gbf[both, :] = in_part.astype(BF)
                gbf[rows[2], :] = out_part.astype(BF)

    row_i = lax.broadcasted_iota(jnp.int32, (QB, QB), 0)
    col_i = lax.broadcasted_iota(jnp.int32, (QB, QB), 1)

    def attend(q, keys, vals, i, own, lse_ref, h):
        diag = pl.ds(i * QB, QB)
        if own:
            lo, n = 0, i * QB
        else:
            lo, n = (i + 1) * QB, TOK - (i + 1) * QB
        sd = nt(q, keys(diag))
        sd = jnp.where((col_i <= row_i) if own else (col_i >= row_i), sd, NEG)
        m = jnp.max(sd, axis=1, keepdims=True)
        if n:
            so = nt(q, keys(pl.ds(lo, n)))
            m = jnp.maximum(m, jnp.max(so, axis=1, keepdims=True))
        pd = jnp.exp2((sd - m) * SCALE)
        l = jnp.sum(pd, axis=1, keepdims=True)
        o = nn(pd.astype(BF), vals(diag))
        if n:
            po = jnp.exp2((so - m) * SCALE)
            l = l + jnp.sum(po, axis=1, keepdims=True)
            o = o + nn(po.astype(BF), vals(pl.ds(lo, n)))
        lse = m * SCALE + jnp.log2(l)
        lse_ref[diag, pl.ds(h, 1)] = lse
        return o / l

    def blocks(b):
        return range(b * TOK // QB // 2, (b + 1) * TOK // QB // 2)

    def own(h, b):
        for i in blocks(b):
            tok = pl.ds(i * QB, QB)
            o_own[tok, lanes(h)] = attend(
                aq_v[tok, lanes(h)], lambda r: ak_v[r, lanes(h)], lambda r: av_v[r, lanes(h)],
                i, True, lse_own, h,
            )

    def serve(h, b):
        if h < SERVED:
            q_copy(h, b).wait_recv()
            for i in blocks(b):
                tok = pl.ds(i * QB, QB)
                o_send[h, tok, :] = attend(
                    qn[h, tok, :], lambda r: ak_v[r, lanes(h)], lambda r: av_v[r, lanes(h)],
                    i, False, lse_nb, h,
                ).astype(BF)
            o_copy(h, b).start()
        else:
            n = h - SERVED
            for i in blocks(b):
                tok = pl.ds(i * QB, QB)
                o_recv[h, tok, :] = attend(
                    aq_v[tok, lanes(h)], lambda r: kn[n, r, :], lambda r: vn[n, r, :],
                    i, False, lse_kv, h,
                ).astype(BF)

    lse_own[...] = jnp.zeros_like(lse_own)
    lse_nb[...] = jnp.zeros_like(lse_nb)

    def send_lse():
        for i in range(TOK // HD):
            lse_send[:, pl.ds(i * HD, HD)] = lse_nb[pl.ds(i * HD, HD), :].T[0:8, :]
        lse_copy().start()

    def merge():
        for h in range(SERVED):
            for b in range(2):
                o_copy(h, b).wait_recv()
        lse_copy().wait_recv()
        for i in range(TOK // HD):
            tok = pl.ds(i * HD, HD)
            theirs = jnp.concatenate([lse_recv[:, tok], jnp.zeros((HD - 8, HD), F32)], axis=0).T
            for h in range(HEADS):
                t = theirs[:, h : h + 1] if h < SERVED else lse_kv[tok, h : h + 1]
                t = jnp.where(seq == 0, NEG, t)
                k = 1.0 / (1.0 + jnp.exp2(t - lse_own[tok, h : h + 1]))
                o_own[tok, lanes(h)] = (
                    o_own[tok, lanes(h)] * k + o_recv[h, tok, :].astype(F32) * (1.0 - k)
                )

    squares = []
    stores = []

    def apply(c, first, last):
        base, width, *_ = sizes(c)
        u = nstack[pl.ds(base + 2 * width, width), :].astype(F32)
        squares.append(jnp.sum(u * u, axis=0, keepdims=True))
        if last:
            old = w2_v[...]
            factor = jnp.sqrt(jnp.sum(old * old, axis=0, keepdims=True)) / jnp.sqrt(
                sum(squares) + EPS
            )

        def tokens(i, _):
            tok = pl.ds(i * AB if last else pl.multiple_of(i * AB, AB), AB)
            q = fq_v[tok, :]
            pre = nt(q, nstack[pl.ds(base, 2 * width), :])
            pg, pu = pre[:, :width], pre[:, width:]
            hid = (pg * jax.nn.sigmoid(pg) * pu).astype(BF)
            o = nn(hid, nstack[pl.ds(base + 2 * width, width), :])
            if not first:
                o = acc[tok, :] + o
            if last:
                res[tok, :] = (o_own[tok, :] + o * factor).astype(BF)
            else:
                acc[tok, :] = o
            return 0

        if not last:
            lax.fori_loop(0, TOK // AB, tokens, 0)
        else:
            for i in range(TOK // AB):
                tokens(i, 0)
                stores.append(
                    pltpu.make_async_copy(
                        res.at[pl.ds(i * AB, AB)], out.at[pl.ds(i * AB, AB)], st_sem.at[i]
                    )
                )
                stores[-1].start()

    waited = set()

    def loaded(*names):
        for i in names:
            if i not in waited:
                waited.add(i)
                loads[i].wait()

    applied = [0]
    grown = []
    merged = [False]
    left = set((h, b) for h in range(SERVED) for b in range(2))
    for token in ORDER:
        kind, first = token[0], int(token[1:2] or 0)
        b = int(token[2]) if len(token) > 2 else 0
        if kind == "q":
            q_copy(first, b).start()
        elif kind == "v":
            for cp in kv_copies(first, b):
                cp.start()
        elif kind == "o":
            loaded(6, 7, 8)
            own(first, b)
        elif kind == "s":
            loaded(6, 7, 8)
            if first >= SERVED:
                for part_ in (1, 0):
                    if part_ >= b and (first, part_) not in waited:
                        waited.add((first, part_))
                        for cp in kv_copies(first, part_):
                            cp.wait_recv()
            serve(first, b)
            if first < SERVED:
                left.discard((first, b))
                if not left:
                    send_lse()
        elif kind == "G":
            loaded(*range(6))
            if not grown:
                for i in (10, 11, 12, 6, 7, 8, 9):
                    loads[i].start()
            else:
                loaded(10, 11, 12)
            grown.append(first)
            prepare(first)
            grads(first)
            rs1_start(first)
        elif kind == "m":
            rs1_mid(first)
        elif kind == "e":
            rs1_end(first)
        elif kind == "r":
            rs2_end(first)
        elif kind == "a":
            ag2_end(first)
        elif kind == "f":
            ag1_fwd(first)
        elif kind == "M":
            merge()
        elif kind == "P":
            loaded(9)
            ag1_end(first)
            applied[0] += 1
            apply(first, applied[0] == 1, applied[0] == len(CHUNKS))

    for cp in stores:
        cp.wait()
    for h in range(HEADS):
        for b in range(2):
            if h < SERVED:
                q_copy(h, b).wait_send()
                o_copy(h, b).wait_send()
            else:
                for cp in kv_copies(h, b):
                    cp.wait_send()
    lse_copy().wait_send()
    for c in range(len(CHUNKS)):
        for cp in (*rs1_copies(c), *rs2_copies(c), *ag2_copies(c), *ag1_copies(c)):
            cp.wait_send()


def hand_on(src, dst):
    dst[...] = src[...]


def shards(attn_q, attn_k, attn_v, fast_q, fast_k, fast_v, rates, fast_gate, fast_up, fast_down):
    rows = TOK
    act = pltpu.VMEM((rows, FWD), BF)
    weight = pltpu.VMEM((FWD, FWD), F32)
    n = len(CHUNKS)
    half = [3 * w // 8 for _, w, _ in CHUNKS]
    share = max(up16(3 * w // 16) for _, w, _ in CHUNKS)
    scratch = [
        act, act, act, act, act, act, pltpu.VMEM((1, rows), F32), weight, weight, weight,
        pltpu.VMEM((3 * FWD, FWD), F32),
        pltpu.VMEM((3 * FWD, FWD), BF),
        pltpu.VMEM((3 * FWD, FWD), F32),
        pltpu.VMEM((3 * FWD, FWD), BF),
        *[pltpu.VMEM((6, h, FWD), BF) for h in half],
        *[pltpu.VMEM((2, h, FWD), BF) for h in half],
        pltpu.VMEM((2 * max(half), FWD), F32),
        pltpu.VMEM((n, 3, share, FWD), BF),
        pltpu.VMEM((n, 3, share, FWD), BF),
        pltpu.VMEM((n, share, FWD), BF),
        pltpu.VMEM((n, 3, share, FWD), BF),
        pltpu.VMEM((3 * FWD, FWD), BF),
        pltpu.VMEM((SERVED, rows, HD), BF),
        pltpu.VMEM((KV_HEADS, rows, HD), BF),
        pltpu.VMEM((KV_HEADS, rows, HD), BF),
        pltpu.VMEM((SERVED, rows, HD), BF),
        pltpu.VMEM((HEADS, rows, HD), BF),
        pltpu.VMEM((rows, FWD), F32),
        pltpu.VMEM((rows, HD), F32),
        pltpu.VMEM((rows, HD), F32),
        pltpu.VMEM((rows, HD), F32),
        pltpu.VMEM((8, rows), F32),
        pltpu.VMEM((8, rows), F32),
        pltpu.VMEM((rows, FWD), F32),
        pltpu.VMEM((3 * 256, TB), BF),
        act,
        pltpu.SemaphoreType.DMA((13,)),
        pltpu.SemaphoreType.DMA((TOK // AB,)),
        *[pltpu.SemaphoreType.DMA((SERVED, 2))] * 4,
        *[pltpu.SemaphoreType.DMA((KV_HEADS, 2, 2))] * 2,
        pltpu.SemaphoreType.DMA((1,)),
        pltpu.SemaphoreType.DMA((1,)),
        pltpu.SemaphoreType.DMA((n, 18)),
        pltpu.SemaphoreType.DMA((n, 18)),
    ]
    square = fast_gate.reshape(FWD, FWD), fast_up.reshape(FWD, FWD), fast_down.reshape(FWD, FWD)
    out = pl.pallas_call(
        kernel,
        out_shape=jax.ShapeDtypeStruct((rows, FWD), BF),
        in_specs=[pl.BlockSpec(memory_space=pl.ANY)] * 10,
        out_specs=pl.BlockSpec(memory_space=pl.ANY),
        scratch_shapes=scratch,
        compiler_params=pltpu.CompilerParams(
            collective_id=0, has_side_effects=True, vmem_limit_bytes=60 << 20
        ),
    )(attn_q, attn_k, attn_v, fast_q, fast_k, fast_v, rates.reshape(1, rows), *square)
    block = pl.BlockSpec((rows // PIECES, FWD), lambda i: (i, 0))
    return pl.pallas_call(
        hand_on,
        grid=(PIECES,),
        out_shape=jax.ShapeDtypeStruct((rows, FWD), BF),
        in_specs=[block],
        out_specs=block,
    )(out)


def solution(mesh):
    placed = (P("seq", "head"),) * 7 + (P("head", None, None),) * 3
    return jax.shard_map(
        shards, mesh=mesh, in_specs=placed, out_specs=P("seq", "head"), check_vma=False
    )
```
